128 devices in a mesh: batch: 2 (over z_lo), seq: 64 (over y, z_hi, x, core).
Axes of the slice: x: 4, y: 4, z: 4 (z_hi: 2, z_lo: 2; z = z_hi * 2 + z_lo), core: 2. Of those that a mesh axis runs over, the one named last changes fastest.
Arguments:
- query_gate: float32 [4, 16384, 128], P('batch', 'seq'), may hold values from -6 to 6
- key_gate: float32 [4, 16384, 128], P('batch', 'seq'), may hold values from -6 to 6
- value_input: float32 [4, 16384, 128], P('batch', 'seq'), may hold values from -6 to 6
- filters: float32 [128, 16384], P('seq'), may hold values from -1 to 1, as said below
- skip_gain: float32 [128], replicated, may hold values from 0.5 to 1.5
- cotangent: float32 [4, 16384, 128], P('batch', 'seq'), may hold values from -6 to 6
Outputs:
- output: float32 [4, 16384, 128], P('batch', 'seq')
- query_grad: float32 [4, 16384, 128], P('batch', 'seq')
- key_grad: float32 [4, 16384, 128], P('batch', 'seq')
- value_grad: float32 [4, 16384, 128], P('batch', 'seq')
- filter_grad: float32 [128, 16384], P('seq', 'batch')
The draws below stay inside these ranges and needn't reach their ends.
Inputs may be any that keep to these rules, and one draw needn't show every extreme that they name: `filters`: each channel's filter has a sum of squares of one.
All inputs are finite; a program needn't handle non-finite values.
Results may differ from the reference program's by a relative error of at most 0.0001.
Values sent between devices are 32-bit elements; how exact they have to be, the bound alone decides.
A program may use at most 128 MiB of HBM per device.

```python
import math
import jax
import jax.numpy as jnp
from jax import lax

CHAN = 128
LEN = 16384
BATCH = 4


def draw_filters(key, part):
    key_noise = jax.random.fold_in(key, 11)
    key_decay = jax.random.fold_in(key, 12)
    position_index = jnp.arange(LEN, dtype=jnp.float32)
    decay_spans = LEN * jnp.exp(jax.random.uniform(key_decay, (CHAN, 1), jnp.float32, math.log(0.002), math.log(4.0)))
    envelope = jnp.exp(-position_index[None, :] / decay_spans)
    noise_draw = jax.random.normal(key_noise, (CHAN, LEN), jnp.float32)
    raw_filter = noise_draw * envelope
    return raw_filter / jnp.sqrt(jnp.sum(raw_filter * raw_filter, axis=1, keepdims=True))


def block_scale(rng, dims, split, low, high):
    factor_of = 1.0
    for position, shards_of in split:
        steps = jax.random.uniform(jax.random.fold_in(jax.random.fold_in(rng, 6), position), (shards_of,), jnp.float32, low / len(split), high / len(split))
        factor_of = factor_of * jnp.repeat(jnp.exp(steps), dims[position] // shards_of).reshape((-1,) + (1,) * (len(dims) - 1 - position))
    return factor_of


def bell_draw(own_key, dims, spread, bound, pieces=(), held_as=jnp.bfloat16):
    result = jax.random.normal(own_key, dims, jnp.float32) * spread
    if len(pieces) > 0:
        result = block_scale(own_key, dims, pieces, -0.22, 0.18) * result
    return jnp.clip(result, min=-bound, max=bound).astype(held_as)


def setup_inputs(seed: int = 0) -> dict:
    key_list = jax.random.split(jax.random.key(seed), 7)
    query_gate = bell_draw(key_list[0], (BATCH, LEN, CHAN), 1.0, 6.0, ((0, 2), (1, 64)), jnp.float32)
    key_gate = bell_draw(key_list[1], (BATCH, LEN, CHAN), 1.0, 6.0, ((0, 2), (1, 64)), jnp.float32)
    value_input = bell_draw(key_list[2], (BATCH, LEN, CHAN), 1.0, 6.0, ((0, 2), (1, 64)), jnp.float32)
    filters = draw_filters(jax.random.fold_in(key_list[6], 71), 0)
    skip_gain = jnp.clip(jax.random.uniform(key_list[4], (CHAN,), jnp.float32, 0.5, 1.5), 0.5, 1.5)
    cotangent = bell_draw(key_list[5], (BATCH, LEN, CHAN), 1.0, 6.0, ((0, 2), (1, 64)), jnp.float32)
    return {"query_gate": query_gate, "key_gate": key_gate, "value_input": value_input, "filters": filters, "skip_gain": skip_gain, "cotangent": cotangent}


def reference(query_gate, key_gate, value_input, filters, skip_gain, cotangent):
    full_length = 2 * LEN
    mixed = key_gate * value_input
    upstream = cotangent * query_gate
    mixed_spectrum = jnp.fft.rfft(jnp.transpose(mixed, (0, 2, 1)), n=full_length, axis=-1)
    upstream_spectrum = jnp.fft.rfft(jnp.transpose(upstream, (0, 2, 1)), n=full_length, axis=-1)
    filter_spectrum = jnp.fft.rfft(filters, n=full_length, axis=-1)
    convolved = jnp.fft.irfft(mixed_spectrum * filter_spectrum[None], n=full_length, axis=-1)[..., :LEN]
    back_term = jnp.fft.irfft(jnp.conj(filter_spectrum)[None] * upstream_spectrum, n=full_length, axis=-1)[..., :LEN]
    filter_sum = lax.optimization_barrier(jnp.sum(jnp.conj(mixed_spectrum) * upstream_spectrum, axis=0))
    filter_grad = jnp.fft.irfft(filter_sum, n=full_length, axis=-1)[..., :LEN] / math.sqrt(LEN)
    hidden_state = jnp.transpose(convolved, (0, 2, 1)) + skip_gain * mixed
    output = query_gate * hidden_state
    query_grad = cotangent * hidden_state
    mixed_grad = jnp.transpose(back_term, (0, 2, 1)) + skip_gain * upstream
    key_grad = mixed_grad * value_input
    value_grad = mixed_grad * key_gate
    return (output, query_grad, key_grad, value_grad, filter_grad)
```

```python
import functools

import jax
import jax.numpy as jnp
import numpy as np
from jax import lax
from jax.experimental import pallas as pl
from jax.experimental.pallas import tpu as pltpu
from jax.sharding import PartitionSpec as P

MESH = pl.DeviceIdType.MESH
F32 = jnp.float32
BF16 = jnp.bfloat16

PEERS = 64
ROWS = 8
K1 = 128
K2 = 256
FULL = K1 * K2


def split_np(table):
    hi = table.astype(BF16)
    lo = (table - hi.astype(np.float64)).astype(BF16)
    return hi, lo


def make_tables():
    k1 = np.arange(K1)
    n1 = np.arange(PEERS)
    n2 = np.arange(K2)
    ang1 = 2.0 * np.pi * (np.outer(k1, n1) % K1) / K1
    c1, s1 = np.cos(ang1), np.sin(ang1)
    left = np.block([[c1, s1], [-s1, c1]])
    left_hi, left_lo = split_np(left)
    left_a = np.concatenate([left_hi, left_hi], axis=1)
    left_f = np.concatenate(
        [left_hi[:, :PEERS], left_hi[:, :PEERS], left_lo[:, :PEERS]], axis=1
    )
    inv_hi, inv_lo = split_np(left.T / FULL)
    inv = np.concatenate([inv_hi, inv_lo], axis=0)
    ang2 = 2.0 * np.pi * (np.outer(n2, n2) % K2) / K2
    c2, s2 = np.cos(ang2), np.sin(ang2)
    right_hi, right_lo = split_np(np.block([[c2, -s2], [s2, c2]]))
    angt = 2.0 * np.pi * (np.outer(k1, n2) % FULL) / FULL
    twist = np.concatenate([np.cos(angt), np.sin(angt)], axis=0).astype(np.float32)
    return (left_a, left_lo, left_f, inv, right_hi, right_lo, twist)


def halves(x):
    hi = x.astype(BF16)
    lo = (x - hi.astype(F32)).astype(BF16)
    return hi, lo


def dot(a, b):
    return jnp.dot(a, b, preferred_element_type=F32)


def turn_forward(section, twist):
    re, im = section[:K1], section[K1:]
    tc, ts = twist[:K1], twist[K1:]
    return re * tc + im * ts, im * tc - re * ts


def turn_inverse(re, im, twist):
    tc, ts = twist[:K1], twist[K1:]
    return re * tc - im * ts, im * tc + re * ts


def put_pair(pair_ref, channel, first, second):
    for part, value in enumerate((first, second)):
        hi, lo = halves(value)
        pair_ref[channel * K1 : (channel + 1) * K1, part * K2 : (part + 1) * K2] = hi
        pair_ref[
            2 * K1 + channel * K1 : 2 * K1 + (channel + 1) * K1, part * K2 : (part + 1) * K2
        ] = lo


def second_stage(pair_ref, right_hi, right_lo):
    wide = dot(pair_ref[...], right_hi[...])
    return wide[: 2 * K1] + wide[2 * K1 :] + dot(pair_ref[: 2 * K1, :], right_lo[...])


def gather_rows(block_ref, row):
    return block_ref[pl.ds(row, PEERS, stride=ROWS), :]


def forward(block_ref, spec_ref, pair_ref, tables):
    left_a, left_lo, _, _, right_hi, right_lo, twist = tables
    for c in range(2):
        rows = [
            jnp.concatenate(
                [gather_rows(block_ref, c * 4 + b * 2), gather_rows(block_ref, c * 4 + b * 2 + 1)],
                axis=1,
            )
            for b in range(2)
        ]
        hi, lo = halves(jnp.concatenate(rows, axis=0))
        section = dot(left_a[...], jnp.concatenate([hi, lo], axis=0)) + dot(left_lo[...], hi)
        put_pair(pair_ref, c, *turn_forward(section, twist))
    spec_ref[...] = second_stage(pair_ref, right_hi, right_lo)


def forward_filters(rows_ref, spec_ref, pair_ref, tables):
    _, _, left_f, _, right_hi, right_lo, twist = tables
    for c in range(2):
        hi, lo = halves(rows_ref[c * PEERS : (c + 1) * PEERS, :])
        section = dot(left_f[...], jnp.concatenate([hi, lo, hi], axis=0))
        put_pair(pair_ref, c, *turn_forward(section, twist))
    spec_ref[...] = second_stage(pair_ref, right_hi, right_lo)


def multiply(left_ref, right_ref, c, conjugate_left):
    rows = slice(c * K1, (c + 1) * K1)
    lr, li = left_ref[rows, :K2], left_ref[rows, K2:]
    rr, ri = right_ref[rows, :K2], right_ref[rows, K2:]
    if conjugate_left:
        return lr * rr + li * ri, lr * ri - li * rr
    return lr * rr - li * ri, lr * ri + li * rr


def inverse(left_ref, right_ref, conjugate_left, pair_ref, wide_ref, tables, real_only):
    _, _, _, inv, right_hi, right_lo, twist = tables
    for c in range(2):
        re, im = multiply(left_ref, right_ref, c, conjugate_left)
        put_pair(pair_ref, c, im, re)
    wide_ref[...] = second_stage(pair_ref, right_hi, right_lo)
    results = []
    for c in range(2):
        rows = slice(c * K1, (c + 1) * K1)
        re, im = turn_inverse(wide_ref[rows, K2:], wide_ref[rows, :K2], twist)
        hi, lo = halves(jnp.concatenate([re, im], axis=0))
        if real_only:
            results.append(
                dot(inv[:PEERS, :], hi) + dot(inv[2 * PEERS : 3 * PEERS, :], hi) + dot(inv[:PEERS, :], lo)
            )
        else:
            both = dot(inv[...], hi)
            results.append(both[:K1] + both[K1:] + dot(inv[:K1, :], lo))
    return results


def main_kernel(
    query_hbm, key_hbm, value_hbm, cotangent_hbm, filters_hbm, *rest
):
    table_hbm, rest = rest[:7], rest[7:]
    conv_out, back_out, lag_own_out, lag_other_out = rest[:4]
    rest = rest[4:]
    query, key, value, cotangent, filters = rest[:5]
    tables, rest = rest[5:12], rest[12:]
    (
        mixed_send, up_send, mixed_got, up_got, conv_send, back_send,
        filter_rows, filter_spec, mixed_spec, up_spec, pair, wide, lag, lag_got,
        load_sem, send_sem, recv_sem, lag_sem, own_sem,
    ) = rest
    b = lax.axis_index("batch")
    s = lax.axis_index("seq")

    loads = [
        pltpu.make_async_copy(src, dst, load_sem.at[i])
        for i, (src, dst) in enumerate(
            zip(
                (key_hbm, value_hbm, query_hbm, cotangent_hbm, filters_hbm) + tuple(table_hbm),
                (key, value, query, cotangent, filters) + tuple(tables),
            )
        )
    ]
    for load in loads:
        load.start()

    def peer(i):
        turn = lax.rem(i - 1 + s * 17, PEERS - 1) + 1
        return lax.rem(s + turn * 23, PEERS)

    barrier = pltpu.get_barrier_semaphore()

    def greet(i, carry):
        pl.semaphore_signal(barrier, inc=1, device_id=(b, peer(i)), device_id_type=MESH)
        return carry

    lax.fori_loop(1, PEERS, greet, 0)
    pl.semaphore_signal(barrier, inc=1, device_id=(1 - b, s), device_id_type=MESH)

    for first, second, left, right, target in (
        (0, 1, key, value, mixed_send),
        (2, 3, query, cotangent, up_send),
    ):
        loads[first].wait()
        loads[second].wait()
        for bb in range(2):
            for half in range(2):
                tokens = slice(half * 128, (half + 1) * 128)
                product = left[bb, tokens, :] * right[bb, tokens, :]
                target[pl.ds(bb * 2 + half, 128, stride=4), :] = product.T

    pl.semaphore_wait(barrier, PEERS)

    def block(i):
        return pl.ds(pl.multiple_of(i * ROWS, ROWS), ROWS)

    def send(source, target, k):
        def one(i, carry):
            d = peer(i)
            pltpu.make_async_remote_copy(
                src_ref=source.at[block(d)],
                dst_ref=target.at[block(s)],
                send_sem=send_sem.at[k],
                recv_sem=recv_sem.at[k],
                device_id=(b, d),
                device_id_type=MESH,
            ).start()
            return carry

        lax.fori_loop(1, PEERS, one, 0)

    def settled(source, target, k):
        rows = pl.ds(0, (PEERS - 1) * ROWS)
        return pltpu.make_async_remote_copy(
            src_ref=source.at[rows],
            dst_ref=target.at[rows],
            send_sem=send_sem.at[k],
            recv_sem=recv_sem.at[k],
            device_id=(1 - b, s),
            device_id_type=MESH,
        )

    send(mixed_send, mixed_got, 0)
    send(up_send, up_got, 1)
    mixed_got[block(s), :] = mixed_send[block(s), :]
    up_got[block(s), :] = up_send[block(s), :]

    for load in loads[4:]:
        load.wait()
    for c in range(2):
        for n1 in range(PEERS):
            filter_rows[c * PEERS + n1 : c * PEERS + n1 + 1, :] = filters[
                c : c + 1, n1 * K2 : (n1 + 1) * K2
            ]
    forward_filters(filter_rows, filter_spec, pair, tables)

    def spread(results, target):
        for c in range(2):
            for bb in range(2):
                for half in range(2):
                    target[pl.ds(c * 4 + bb * 2 + half, PEERS, stride=ROWS), :] = results[c][
                        bb * PEERS : (bb + 1) * PEERS, half * 128 : (half + 1) * 128
                    ]

    settled(mixed_send, mixed_got, 0).wait_recv()
    forward(mixed_got, mixed_spec, pair, tables)
    spread(inverse(mixed_spec, filter_spec, False, pair, wide, tables, False), conv_send)
    send(conv_send, conv_out, 2)
    own_conv = pltpu.make_async_copy(conv_send.at[block(s)], conv_out.at[block(s)], own_sem.at[0])
    own_conv.start()

    settled(up_send, up_got, 1).wait_recv()
    forward(up_got, up_spec, pair, tables)
    spread(inverse(filter_spec, up_spec, True, pair, wide, tables, False), back_send)
    send(back_send, back_out, 3)
    own_back = pltpu.make_async_copy(back_send.at[block(s)], back_out.at[block(s)], own_sem.at[1])
    own_back.start()

    results = inverse(mixed_spec, up_spec, True, pair, wide, tables, True)
    for half in range(2):
        for c in range(2):
            lag[half, c * 32 : (c + 1) * 32, :] = results[c][half * 32 : (half + 1) * 32, :]
    lag_copy = pltpu.make_async_remote_copy(
        src_ref=lag.at[1 - b],
        dst_ref=lag_got,
        send_sem=lag_sem.at[0],
        recv_sem=lag_sem.at[1],
        device_id=(1 - b, s),
        device_id_type=MESH,
    )
    lag_copy.start()
    own_lag = pltpu.make_async_copy(lag.at[b], lag_own_out, own_sem.at[2])
    own_lag.start()
    lag_copy.wait_recv()
    other_lag = pltpu.make_async_copy(lag_got, lag_other_out, own_sem.at[3])
    other_lag.start()

    settled(mixed_send, mixed_got, 0).wait_send()
    settled(up_send, up_got, 1).wait_send()
    settled(conv_send, conv_out, 2).wait()
    settled(back_send, back_out, 3).wait()
    lag_copy.wait_send()
    own_conv.wait()
    own_back.wait()
    own_lag.wait()
    other_lag.wait()


def final_kernel(
    conv, back, lag_own, lag_other, query, key, value, cotangent, skip,
    output, query_grad, key_grad, value_grad, filter_grad,
):
    gain = skip[...]
    for bb in range(2):
        for half in range(2):
            tokens = slice(half * 128, (half + 1) * 128)
            q, k = query[bb, tokens, :], key[bb, tokens, :]
            v, g = value[bb, tokens, :], cotangent[bb, tokens, :]
            rows = pl.ds(bb * 2 + half, 128, stride=4)
            hidden = conv[rows, :].T + gain * (k * v)
            output[bb, tokens, :] = q * hidden
            query_grad[bb, tokens, :] = g * hidden
            mixed_grad = back[rows, :].T + gain * (g * q)
            key_grad[bb, tokens, :] = mixed_grad * v
            value_grad[bb, tokens, :] = mixed_grad * k
    total = (lag_own[...] + lag_other[...]) * (1.0 / 128.0)
    for c in range(2):
        for n in range(32):
            filter_grad[c : c + 1, n * K2 : (n + 1) * K2] = total[c * 32 + n : c * 32 + n + 1, :]


def per_device(query, key, value, filters, skip, cotangent):
    tables = [jnp.asarray(t) for t in make_tables()]
    message = (PEERS * ROWS, 128)
    any_space = pl.BlockSpec(memory_space=pl.ANY)
    in_vmem = pl.BlockSpec(memory_space=pltpu.VMEM)
    vmem = pltpu.VMEM
    tokens = query.shape
    conv, back, lag_own, lag_other = pl.pallas_call(
        main_kernel,
        out_shape=(
            jax.ShapeDtypeStruct(message, F32),
            jax.ShapeDtypeStruct(message, F32),
            jax.ShapeDtypeStruct((64, K2), F32),
            jax.ShapeDtypeStruct((64, K2), F32),
        ),
        in_specs=[any_space] * 12,
        out_specs=(any_space,) * 4,
        scratch_shapes=[vmem(tokens, F32)] * 4
        + [vmem(filters.shape, F32)]
        + [vmem(t.shape, t.dtype) for t in tables]
        + [vmem(message, F32)] * 6
        + [vmem((2 * PEERS, K2), F32)]
        + [vmem((2 * K1, 2 * K2), F32)] * 3
        + [vmem((4 * K1, 2 * K2), BF16), vmem((2 * K1, 2 * K2), F32)]
        + [vmem((2, 64, K2), F32), vmem((64, K2), F32)]
        + [
            pltpu.SemaphoreType.DMA((12,)),
            pltpu.SemaphoreType.DMA((4,)),
            pltpu.SemaphoreType.DMA((4,)),
            pltpu.SemaphoreType.DMA((2,)),
            pltpu.SemaphoreType.DMA((4,)),
        ],
        compiler_params=pltpu.CompilerParams(
            collective_id=0, has_side_effects=True, vmem_limit_bytes=40 * 1024 * 1024
        ),
        name="spectral_exchange",
    )(query, key, value, cotangent, filters, *tables)
    block = jax.ShapeDtypeStruct(tokens, F32)
    return pl.pallas_call(
        final_kernel,
        out_shape=(block, block, block, block, jax.ShapeDtypeStruct((2, 32 * K2), F32)),
        in_specs=[in_vmem] * 9,
        out_specs=(in_vmem,) * 5,
        name="gates",
    )(conv, back, lag_own, lag_other, query, key, value, cotangent, skip.reshape(1, -1))


def solution(mesh):
    rows = P("batch", "seq", None)
    return jax.shard_map(
        per_device,
        mesh=mesh,
        in_specs=(rows, rows, rows, P("seq", None), P(), rows),
        out_specs=(rows, rows, rows, rows, P("seq", "batch")),
        check_vma=False,
    )
```

```python
import functools

import jax
import jax.numpy as jnp
import numpy as np
from jax import lax
from jax.experimental import pallas as pl
from jax.experimental.pallas import tpu as pltpu
from jax.sharding import PartitionSpec as P

MESH = pl.DeviceIdType.MESH
F32 = jnp.float32
BF16 = jnp.bfloat16

PEERS = 64
ROWS = 8
K1 = 128
K2 = 256
FULL = K1 * K2


def split_np(table):
    hi = table.astype(BF16)
    lo = (table - hi.astype(np.float64)).astype(BF16)
    return hi, lo


def make_tables():
    k1 = np.arange(K1)
    n1 = np.arange(PEERS)
    n2 = np.arange(K2)
    ang1 = 2.0 * np.pi * (np.outer(k1, n1) % K1) / K1
    c1, s1 = np.cos(ang1), np.sin(ang1)
    left = np.block([[c1, s1], [-s1, c1]])
    left_hi, left_lo = split_np(left)
    left_a = np.concatenate([left_hi, left_hi], axis=1)
    left_f = np.concatenate(
        [left_hi[:, :PEERS], left_hi[:, :PEERS], left_lo[:, :PEERS]], axis=1
    )
    inv_hi, inv_lo = split_np(left.T / FULL)
    inv = np.concatenate([inv_hi, inv_lo], axis=0)
    ang2 = 2.0 * np.pi * (np.outer(n2, n2) % K2) / K2
    c2, s2 = np.cos(ang2), np.sin(ang2)
    right_hi, right_lo = split_np(np.block([[c2, -s2], [s2, c2]]))
    angt = 2.0 * np.pi * (np.outer(k1, n2) % FULL) / FULL
    twist = np.concatenate([np.cos(angt), np.sin(angt)], axis=0).astype(np.float32)
    return (left_a, left_lo, left_f, inv, right_hi, right_lo, twist)


def halves(x):
    hi = x.astype(BF16)
    lo = (x - hi.astype(F32)).astype(BF16)
    return hi, lo


def dot(a, b):
    return jnp.dot(a, b, preferred_element_type=F32)


def turn_forward(section, twist):
    re, im = section[:K1], section[K1:]
    tc, ts = twist[:K1], twist[K1:]
    return re * tc + im * ts, im * tc - re * ts


def turn_inverse(re, im, twist):
    tc, ts = twist[:K1], twist[K1:]
    return re * tc - im * ts, im * tc + re * ts


def put_pair(pair_ref, channel, first, second):
    for part, value in enumerate((first, second)):
        hi, lo = halves(value)
        pair_ref[channel * K1 : (channel + 1) * K1, part * K2 : (part + 1) * K2] = hi
        pair_ref[
            2 * K1 + channel * K1 : 2 * K1 + (channel + 1) * K1, part * K2 : (part + 1) * K2
        ] = lo


def second_stage(pair_ref, right_hi, right_lo):
    wide = dot(pair_ref[...], right_hi[...])
    return wide[: 2 * K1] + wide[2 * K1 :] + dot(pair_ref[: 2 * K1, :], right_lo[...])


def gather_rows(block_ref, row):
    return block_ref[pl.ds(row, PEERS, stride=ROWS), :]


def forward(block_ref, spec_ref, pair_ref, tables):
    left_a, left_lo, _, _, right_hi, right_lo, twist = tables
    for c in range(2):
        rows = [
            jnp.concatenate(
                [gather_rows(block_ref, c * 4 + b * 2), gather_rows(block_ref, c * 4 + b * 2 + 1)],
                axis=1,
            )
            for b in range(2)
        ]
        hi, lo = halves(jnp.concatenate(rows, axis=0))
        section = dot(left_a[...], jnp.concatenate([hi, lo], axis=0)) + dot(left_lo[...], hi)
        put_pair(pair_ref, c, *turn_forward(section, twist))
    spec_ref[...] = second_stage(pair_ref, right_hi, right_lo)


def forward_filters(rows_ref, spec_ref, pair_ref, tables):
    _, _, left_f, _, right_hi, right_lo, twist = tables
    for c in range(2):
        hi, lo = halves(rows_ref[c * PEERS : (c + 1) * PEERS, :])
        section = dot(left_f[...], jnp.concatenate([hi, lo, hi], axis=0))
        put_pair(pair_ref, c, *turn_forward(section, twist))
    spec_ref[...] = second_stage(pair_ref, right_hi, right_lo)


def multiply(left_ref, right_ref, c, conjugate_left):
    rows = slice(c * K1, (c + 1) * K1)
    lr, li = left_ref[rows, :K2], left_ref[rows, K2:]
    rr, ri = right_ref[rows, :K2], right_ref[rows, K2:]
    if conjugate_left:
        return lr * rr + li * ri, lr * ri - li * rr
    return lr * rr - li * ri, lr * ri + li * rr


def inverse(left_ref, right_ref, conjugate_left, pair_ref, wide_ref, tables, real_only):
    _, _, _, inv, right_hi, right_lo, twist = tables
    for c in range(2):
        re, im = multiply(left_ref, right_ref, c, conjugate_left)
        put_pair(pair_ref, c, im, re)
    wide_ref[...] = second_stage(pair_ref, right_hi, right_lo)
    results = []
    for c in range(2):
        rows = slice(c * K1, (c + 1) * K1)
        re, im = turn_inverse(wide_ref[rows, K2:], wide_ref[rows, :K2], twist)
        hi, lo = halves(jnp.concatenate([re, im], axis=0))
        if real_only:
            results.append(
                dot(inv[:PEERS, :], hi) + dot(inv[2 * PEERS : 3 * PEERS, :], hi) + dot(inv[:PEERS, :], lo)
            )
        else:
            both = dot(inv[...], hi)
            results.append(both[:K1] + both[K1:] + dot(inv[:K1, :], lo))
    return results


def main_kernel(
    query_hbm, key_hbm, value_hbm, cotangent_hbm, filters_hbm, *rest
):
    table_hbm, rest = rest[:7], rest[7:]
    conv_out, back_out, lag_own_out, lag_other_out = rest[:4]
    rest = rest[4:]
    query, key, value, cotangent, filters = rest[:5]
    tables, rest = rest[5:12], rest[12:]
    (
        mixed_send, up_send, mixed_got, up_got, conv_send, back_send,
        filter_rows, filter_spec, mixed_spec, up_spec, pair, wide, lag, lag_got,
        load_sem, send_sem, recv_sem, lag_sem, own_sem,
    ) = rest
    b = lax.axis_index("batch")
    s = lax.axis_index("seq")

    loads = [
        pltpu.make_async_copy(src, dst, load_sem.at[i])
        for i, (src, dst) in enumerate(
            zip(
                (key_hbm, value_hbm, query_hbm, cotangent_hbm, filters_hbm) + tuple(table_hbm),
                (key, value, query, cotangent, filters) + tuple(tables),
            )
        )
    ]
    for load in loads:
        load.start()

    def peer(i):
        turn = lax.rem(i - 1 + s * 17, PEERS - 1) + 1
        return lax.rem(s + turn * 23, PEERS)

    barrier = pltpu.get_barrier_semaphore()

    def greet(i, carry):
        pl.semaphore_signal(barrier, inc=1, device_id=(b, peer(i)), device_id_type=MESH)
        return carry

    lax.fori_loop(1, PEERS, greet, 0)
    pl.semaphore_signal(barrier, inc=1, device_id=(1 - b, s), device_id_type=MESH)

    for first, second, left, right, target in (
        (0, 1, key, value, mixed_send),
        (2, 3, query, cotangent, up_send),
    ):
        loads[first].wait()
        loads[second].wait()
        for bb in range(2):
            for half in range(2):
                tokens = slice(half * 128, (half + 1) * 128)
                product = left[bb, tokens, :] * right[bb, tokens, :]
                target[pl.ds(bb * 2 + half, 128, stride=4), :] = product.T

    pl.semaphore_wait(barrier, PEERS)

    def block(i):
        return pl.ds(pl.multiple_of(i * ROWS, ROWS), ROWS)

    def send(source, target, k):
        def one(i, carry):
            d = peer(i)
            pltpu.make_async_remote_copy(
                src_ref=source.at[block(d)],
                dst_ref=target.at[block(s)],
                send_sem=send_sem.at[k],
                recv_sem=recv_sem.at[k],
                device_id=(b, d),
                device_id_type=MESH,
            ).start()
            return carry

        lax.fori_loop(1, PEERS, one, 0)

    def settled(source, target, k):
        rows = pl.ds(0, (PEERS - 1) * ROWS)
        return pltpu.make_async_remote_copy(
            src_ref=source.at[rows],
            dst_ref=target.at[rows],
            send_sem=send_sem.at[k],
            recv_sem=recv_sem.at[k],
            device_id=(1 - b, s),
            device_id_type=MESH,
        )

    send(mixed_send, mixed_got, 0)
    send(up_send, up_got, 1)
    mixed_got[block(s), :] = mixed_send[block(s), :]
    up_got[block(s), :] = up_send[block(s), :]

    for load in loads[4:]:
        load.wait()
    for c in range(2):
        for n1 in range(PEERS):
            filter_rows[c * PEERS + n1 : c * PEERS + n1 + 1, :] = filters[
                c : c + 1, n1 * K2 : (n1 + 1) * K2
            ]
    forward_filters(filter_rows, filter_spec, pair, tables)

    def spread(results, target):
        for c in range(2):
            for bb in range(2):
                for half in range(2):
                    target[pl.ds(c * 4 + bb * 2 + half, PEERS, stride=ROWS), :] = results[c][
                        bb * PEERS : (bb + 1) * PEERS, half * 128 : (half + 1) * 128
                    ]

    settled(mixed_send, mixed_got, 0).wait_recv()
    forward(mixed_got, mixed_spec, pair, tables)
    spread(inverse(mixed_spec, filter_spec, False, pair, wide, tables, False), conv_send)
    send(conv_send, conv_out, 2)
    own_conv = pltpu.make_async_copy(conv_send.at[block(s)], conv_out.at[block(s)], own_sem.at[0])
    own_conv.start()

    settled(up_send, up_got, 1).wait_recv()
    forward(up_got, up_spec, pair, tables)
    spread(inverse(filter_spec, up_spec, True, pair, wide, tables, False), back_send)
    send(back_send, back_out, 3)
    own_back = pltpu.make_async_copy(back_send.at[block(s)], back_out.at[block(s)], own_sem.at[1])
    own_back.start()

    results = inverse(mixed_spec, up_spec, True, pair, wide, tables, True)
    for half in range(2):
        for c in range(2):
            lag[half, c * 32 : (c + 1) * 32, :] = results[c][half * 32 : (half + 1) * 32, :]
    lag_copy = pltpu.make_async_remote_copy(
        src_ref=lag.at[1 - b],
        dst_ref=lag_got,
        send_sem=lag_sem.at[0],
        recv_sem=lag_sem.at[1],
        device_id=(1 - b, s),
        device_id_type=MESH,
    )
    lag_copy.start()
    own_lag = pltpu.make_async_copy(lag.at[b], lag_own_out, own_sem.at[2])
    own_lag.start()
    lag_copy.wait_recv()
    other_lag = pltpu.make_async_copy(lag_got, lag_other_out, own_sem.at[3])
    other_lag.start()

    settled(mixed_send, mixed_got, 0).wait_send()
    settled(up_send, up_got, 1).wait_send()
    settled(conv_send, conv_out, 2).wait()
    settled(back_send, back_out, 3).wait()
    lag_copy.wait_send()
    own_conv.wait()
    own_back.wait()
    own_lag.wait()
    other_lag.wait()


def final_kernel(
    conv, back, lag_own, lag_other, query, key, value, cotangent, skip,
    output_hbm, query_grad_hbm, key_grad_hbm, value_grad_hbm, filter_grad_hbm,
    output, query_grad, key_grad, value_grad, filter_grad, out_sem, lag_sem,
):
    gain = skip[...]
    stores = []
    for bb in range(2):
        for half in range(2):
            tokens = slice(half * 128, (half + 1) * 128)
            q, k = query[bb, tokens, :], key[bb, tokens, :]
            v, g = value[bb, tokens, :], cotangent[bb, tokens, :]
            rows = pl.ds(bb * 2 + half, 128, stride=4)
            hidden = conv[rows, :].T + gain * (k * v)
            mixed_grad = back[rows, :].T + gain * (g * q)
            for i, (result, src, dst) in enumerate(
                (
                    (q * hidden, output, output_hbm),
                    (g * hidden, query_grad, query_grad_hbm),
                    (mixed_grad * v, key_grad, key_grad_hbm),
                    (mixed_grad * k, value_grad, value_grad_hbm),
                )
            ):
                src[bb, tokens, :] = result
                store = pltpu.make_async_copy(
                    src.at[bb, tokens], dst.at[bb, tokens], out_sem.at[bb * 2 + half, i]
                )
                store.start()
                stores.append(store)
    total = (lag_own[...] + lag_other[...]) * (1.0 / 128.0)
    for c in range(2):
        for n in range(32):
            filter_grad[c : c + 1, n * K2 : (n + 1) * K2] = total[c * 32 + n : c * 32 + n + 1, :]
    store = pltpu.make_async_copy(filter_grad, filter_grad_hbm, lag_sem)
    store.start()
    stores.append(store)
    for store in stores:
        store.wait()


def per_device(query, key, value, filters, skip, cotangent):
    tables = [jnp.asarray(t) for t in make_tables()]
    message = (PEERS * ROWS, 128)
    in_hbm = pl.BlockSpec(memory_space=pltpu.HBM)
    vmem = pltpu.VMEM
    tokens = query.shape
    operands = (query, key, value, cotangent, filters, *tables)
    conv, back, lag_own, lag_other = pl.pallas_call(
        main_kernel,
        out_shape=(
            jax.ShapeDtypeStruct(message, F32),
            jax.ShapeDtypeStruct(message, F32),
            jax.ShapeDtypeStruct((64, K2), F32),
            jax.ShapeDtypeStruct((64, K2), F32),
        ),
        in_specs=[in_hbm] * 12,
        out_specs=(in_hbm,) * 4,
        scratch_shapes=[vmem(tokens, F32)] * 4
        + [vmem(filters.shape, F32)]
        + [vmem(t.shape, t.dtype) for t in tables]
        + [vmem(message, F32)] * 6
        + [vmem((2 * PEERS, K2), F32)]
        + [vmem((2 * K1, 2 * K2), F32)] * 3
        + [vmem((4 * K1, 2 * K2), BF16), vmem((2 * K1, 2 * K2), F32)]
        + [vmem((2, 64, K2), F32), vmem((64, K2), F32)]
        + [
            pltpu.SemaphoreType.DMA((12,)),
            pltpu.SemaphoreType.DMA((4,)),
            pltpu.SemaphoreType.DMA((4,)),
            pltpu.SemaphoreType.DMA((2,)),
            pltpu.SemaphoreType.DMA((4,)),
        ],
        compiler_params=pltpu.CompilerParams(
            collective_id=0, has_side_effects=True, vmem_limit_bytes=40 * 1024 * 1024
        ),
        name="spectral_exchange",
    )(*[pltpu.with_memory_space_constraint(x, pltpu.HBM) for x in operands])
    block = jax.ShapeDtypeStruct(tokens, F32)
    return pl.pallas_call(
        final_kernel,
        out_shape=(block, block, block, block, jax.ShapeDtypeStruct((2, 32 * K2), F32)),
        in_specs=[pl.BlockSpec(memory_space=pltpu.VMEM)] * 9,
        out_specs=(in_hbm,) * 5,
        scratch_shapes=[vmem(tokens, F32)] * 4
        + [vmem((2, 32 * K2), F32), pltpu.SemaphoreType.DMA((4, 4)), pltpu.SemaphoreType.DMA],
        compiler_params=pltpu.CompilerParams(vmem_limit_bytes=40 * 1024 * 1024),
        name="gates",
    )(conv, back, lag_own, lag_other, query, key, value, cotangent, skip.reshape(1, -1))


def solution(mesh):
    rows = P("batch", "seq", None)
    return jax.shard_map(
        per_device,
        mesh=mesh,
        in_specs=(rows, rows, rows, P("seq", None), P(), rows),
        out_specs=(rows, rows, rows, rows, P("seq", "batch")),
        check_vma=False,
    )
```

```python
import functools

import jax
import jax.numpy as jnp
import numpy as np
from jax import lax
from jax.experimental import pallas as pl
from jax.experimental.pallas import tpu as pltpu
from jax.sharding import PartitionSpec as P

MESH = pl.DeviceIdType.MESH
F32 = jnp.float32
BF16 = jnp.bfloat16

PEERS = 64
ROWS = 8
K1 = 128
K2 = 256
FULL = K1 * K2


AWAY = (0, 1, 2, 1)

SHIFTS = sorted(
    (
        (y, z, x, core)
        for y in range(4)
        for z in range(2)
        for x in range(4)
        for core in range(2)
        if (y, z, x, core) != (0, 0, 0, 0)
    ),
    key=lambda d: -(AWAY[d[0]] + 2 * d[1] + AWAY[d[2]]),
)


def split_np(table):
    hi = table.astype(BF16)
    lo = (table - hi.astype(np.float64)).astype(BF16)
    return hi, lo


def make_tables():
    k1 = np.arange(K1)
    n1 = np.arange(PEERS)
    n2 = np.arange(K2)
    ang1 = 2.0 * np.pi * (np.outer(k1, n1) % K1) / K1
    c1, s1 = np.cos(ang1), np.sin(ang1)
    left = np.block([[c1, s1], [-s1, c1]])
    left_hi, left_lo = split_np(left)
    left_a = np.concatenate([left_hi, left_hi], axis=1)
    left_f = np.concatenate(
        [left_hi[:, :PEERS], left_hi[:, :PEERS], left_lo[:, :PEERS]], axis=1
    )
    inv_hi, inv_lo = split_np(left.T / FULL)
    inv = np.concatenate([inv_hi, inv_lo], axis=0)
    ang2 = 2.0 * np.pi * (np.outer(n2, n2) % K2) / K2
    c2, s2 = np.cos(ang2), np.sin(ang2)
    right_hi, right_lo = split_np(np.block([[c2, -s2], [s2, c2]]))
    angt = 2.0 * np.pi * (np.outer(k1, n2) % FULL) / FULL
    twist = np.concatenate([np.cos(angt), np.sin(angt)], axis=0).astype(np.float32)
    return (left_a, left_lo, left_f, inv, right_hi, right_lo, twist)


def halves(x):
    hi = x.astype(BF16)
    lo = (x - hi.astype(F32)).astype(BF16)
    return hi, lo


def dot(a, b):
    return jnp.dot(a, b, preferred_element_type=F32)


def turn_forward(section, twist):
    re, im = section[:K1], section[K1:]
    tc, ts = twist[:K1], twist[K1:]
    return re * tc + im * ts, im * tc - re * ts


def turn_inverse(re, im, twist):
    tc, ts = twist[:K1], twist[K1:]
    return re * tc - im * ts, im * tc + re * ts


def put_pair(pair_ref, channel, first, second):
    for part, value in enumerate((first, second)):
        hi, lo = halves(value)
        pair_ref[channel * K1 : (channel + 1) * K1, part * K2 : (part + 1) * K2] = hi
        pair_ref[
            2 * K1 + channel * K1 : 2 * K1 + (channel + 1) * K1, part * K2 : (part + 1) * K2
        ] = lo


def second_stage(pair_ref, right_hi, right_lo):
    wide = dot(pair_ref[...], right_hi[...])
    return wide[: 2 * K1] + wide[2 * K1 :] + dot(pair_ref[: 2 * K1, :], right_lo[...])


def gather_rows(block_ref, row):
    return block_ref[pl.ds(row, PEERS, stride=ROWS), :]


def forward(block_ref, spec_ref, pair_ref, tables):
    left_a, left_lo, _, _, right_hi, right_lo, twist = tables
    for c in range(2):
        rows = [
            jnp.concatenate(
                [gather_rows(block_ref, c * 4 + b * 2), gather_rows(block_ref, c * 4 + b * 2 + 1)],
                axis=1,
            )
            for b in range(2)
        ]
        hi, lo = halves(jnp.concatenate(rows, axis=0))
        section = dot(left_a[...], jnp.concatenate([hi, lo], axis=0)) + dot(left_lo[...], hi)
        put_pair(pair_ref, c, *turn_forward(section, twist))
    spec_ref[...] = second_stage(pair_ref, right_hi, right_lo)


def forward_filters(rows_ref, spec_ref, pair_ref, tables):
    _, _, left_f, _, right_hi, right_lo, twist = tables
    for c in range(2):
        hi, lo = halves(rows_ref[c * PEERS : (c + 1) * PEERS, :])
        section = dot(left_f[...], jnp.concatenate([hi, lo, hi], axis=0))
        put_pair(pair_ref, c, *turn_forward(section, twist))
    spec_ref[...] = second_stage(pair_ref, right_hi, right_lo)


def multiply(left_ref, right_ref, c, conjugate_left):
    rows = slice(c * K1, (c + 1) * K1)
    lr, li = left_ref[rows, :K2], left_ref[rows, K2:]
    rr, ri = right_ref[rows, :K2], right_ref[rows, K2:]
    if conjugate_left:
        return lr * rr + li * ri, lr * ri - li * rr
    return lr * rr - li * ri, lr * ri + li * rr


def inverse(left_ref, right_ref, conjugate_left, pair_ref, wide_ref, tables, real_only):
    _, _, _, inv, right_hi, right_lo, twist = tables
    for c in range(2):
        re, im = multiply(left_ref, right_ref, c, conjugate_left)
        put_pair(pair_ref, c, im, re)
    wide_ref[...] = second_stage(pair_ref, right_hi, right_lo)
    results = []
    for c in range(2):
        rows = slice(c * K1, (c + 1) * K1)
        re, im = turn_inverse(wide_ref[rows, K2:], wide_ref[rows, :K2], twist)
        hi, lo = halves(jnp.concatenate([re, im], axis=0))
        if real_only:
            results.append(
                dot(inv[:PEERS, :], hi) + dot(inv[2 * PEERS : 3 * PEERS, :], hi) + dot(inv[:PEERS, :], lo)
            )
        else:
            both = dot(inv[...], hi)
            results.append(both[:K1] + both[K1:] + dot(inv[:K1, :], lo))
    return results


def main_kernel(
    query_hbm, key_hbm, value_hbm, cotangent_hbm, filters_hbm, skip_hbm, *rest
):
    table_hbm, rest = rest[:7], rest[7:]
    output, query_grad, key_grad, value_grad, filter_grad = rest[:5]
    rest = rest[5:]
    query, key, value, cotangent, filters, skip = rest[:6]
    tables, rest = rest[6:13], rest[13:]
    (
        mixed_send, up_send, mixed_got, up_got, conv_send, back_send, conv_got, back_got,
        filter_rows, filter_spec, mixed_spec, up_spec, pair, wide, lag, lag_got,
        load_sem, send_sem, recv_sem, lag_sem,
    ) = rest
    b = lax.axis_index("batch")
    s = lax.axis_index("seq")

    loads = [
        pltpu.make_async_copy(src, dst, load_sem.at[i])
        for i, (src, dst) in enumerate(
            zip(
                (key_hbm, value_hbm, query_hbm, cotangent_hbm, filters_hbm, skip_hbm)
                + tuple(table_hbm),
                (key, value, query, cotangent, filters, skip) + tuple(tables),
            )
        )
    ]
    for load in loads:
        load.start()

    places = (
        [lax.rem(s // 16 + i, 4) * 16 for i in range(4)],
        [lax.rem(s // 8 + i, 2) * 8 for i in range(2)],
        [lax.rem(s // 2 + i, 4) * 2 for i in range(4)],
        [lax.rem(s + i, 2) for i in range(2)],
    )
    peers = [sum(place[i] for place, i in zip(places, shift)) for shift in SHIFTS]

    barrier = pltpu.get_barrier_semaphore()
    for d in peers:
        pl.semaphore_signal(barrier, inc=1, device_id=(b, d), device_id_type=MESH)
    pl.semaphore_signal(barrier, inc=1, device_id=(1 - b, s), device_id_type=MESH)

    for first, second, left, right, target in (
        (0, 1, key, value, mixed_send),
        (2, 3, query, cotangent, up_send),
    ):
        loads[first].wait()
        loads[second].wait()
        for bb in range(2):
            for half in range(2):
                tokens = slice(half * 128, (half + 1) * 128)
                product = left[bb, tokens, :] * right[bb, tokens, :]
                target[pl.ds(bb * 2 + half, 128, stride=4), :] = product.T

    pl.semaphore_wait(barrier, PEERS)

    def block(i):
        return pl.ds(pl.multiple_of(i * ROWS, ROWS), ROWS)

    def send(source, target, k):
        for d in peers:
            pltpu.make_async_remote_copy(
                src_ref=source.at[block(d)],
                dst_ref=target.at[block(s)],
                send_sem=send_sem.at[k],
                recv_sem=recv_sem.at[k],
                device_id=(b, d),
                device_id_type=MESH,
            ).start()
        target[block(s), :] = source[block(s), :]

    def settled(source, target, k):
        rows = pl.ds(0, (PEERS - 1) * ROWS)
        return pltpu.make_async_remote_copy(
            src_ref=source.at[rows],
            dst_ref=target.at[rows],
            send_sem=send_sem.at[k],
            recv_sem=recv_sem.at[k],
            device_id=(1 - b, s),
            device_id_type=MESH,
        )

    send(mixed_send, mixed_got, 0)
    send(up_send, up_got, 1)

    for load in loads[4:]:
        load.wait()
    for c in range(2):
        for n1 in range(PEERS):
            filter_rows[c * PEERS + n1 : c * PEERS + n1 + 1, :] = filters[
                c : c + 1, n1 * K2 : (n1 + 1) * K2
            ]
    forward_filters(filter_rows, filter_spec, pair, tables)

    def spread(results, target):
        for c in range(2):
            for bb in range(2):
                for half in range(2):
                    target[pl.ds(c * 4 + bb * 2 + half, PEERS, stride=ROWS), :] = results[c][
                        bb * PEERS : (bb + 1) * PEERS, half * 128 : (half + 1) * 128
                    ]

    settled(mixed_send, mixed_got, 0).wait_recv()
    forward(mixed_got, mixed_spec, pair, tables)
    spread(inverse(mixed_spec, filter_spec, False, pair, wide, tables, False), conv_send)
    send(conv_send, conv_got, 2)

    settled(up_send, up_got, 1).wait_recv()
    forward(up_got, up_spec, pair, tables)
    spread(inverse(filter_spec, up_spec, True, pair, wide, tables, False), back_send)
    send(back_send, back_got, 3)

    results = inverse(mixed_spec, up_spec, True, pair, wide, tables, True)
    for half in range(2):
        for c in range(2):
            lag[half, c * 32 : (c + 1) * 32, :] = results[c][half * 32 : (half + 1) * 32, :]
    lag_copy = pltpu.make_async_remote_copy(
        src_ref=lag.at[1 - b],
        dst_ref=lag_got,
        send_sem=lag_sem.at[0],
        recv_sem=lag_sem.at[1],
        device_id=(1 - b, s),
        device_id_type=MESH,
    )
    lag_copy.start()

    gain = skip[...]
    parts = [(bb, slice(h * 128, (h + 1) * 128), pl.ds(bb * 2 + h, 128, stride=4)) for bb in range(2) for h in range(2)]
    settled(conv_send, conv_got, 2).wait_recv()
    for bb, tokens, rows in parts:
        hidden = conv_got[rows, :].T + gain * (key[bb, tokens, :] * value[bb, tokens, :])
        output[bb, tokens, :] = query[bb, tokens, :] * hidden
        query_grad[bb, tokens, :] = cotangent[bb, tokens, :] * hidden

    lag_copy.wait_recv()
    total = (lag[b] + lag_got[...]) * (1.0 / 128.0)
    for c in range(2):
        for n in range(32):
            filter_grad[c : c + 1, n * K2 : (n + 1) * K2] = total[c * 32 + n : c * 32 + n + 1, :]
    settled(mixed_send, mixed_got, 0).wait_send()
    settled(up_send, up_got, 1).wait_send()
    settled(conv_send, conv_got, 2).wait_send()
    lag_copy.wait_send()

    settled(back_send, back_got, 3).wait_recv()
    for bb, tokens, rows in parts:
        mixed_grad = back_got[rows, :].T + gain * (cotangent[bb, tokens, :] * query[bb, tokens, :])
        key_grad[bb, tokens, :] = mixed_grad * value[bb, tokens, :]
        value_grad[bb, tokens, :] = mixed_grad * key[bb, tokens, :]
    settled(back_send, back_got, 3).wait_send()


def store_kernel(*refs):
    sources, targets, sem = refs[:5], refs[5:10], refs[10]
    copies = []
    for i in range(5):
        for half in range(2):
            part = (half,) if i < 4 else (slice(None), pl.ds(half * 16 * K2, 16 * K2))
            copies.append(
                pltpu.make_async_copy(sources[i].at[part], targets[i].at[part], sem.at[i, half])
            )
    for copy in copies:
        copy.start()
    for copy in copies:
        copy.wait()


def per_device(query, key, value, filters, skip, cotangent):
    tables = [jnp.asarray(t) for t in make_tables()]
    message = (PEERS * ROWS, 128)
    in_hbm = pl.BlockSpec(memory_space=pltpu.HBM)
    vmem = pltpu.VMEM
    tokens = query.shape
    operands = (query, key, value, cotangent, filters, skip.reshape(1, -1), *tables)
    block = jax.ShapeDtypeStruct(tokens, F32)
    shapes = (block, block, block, block, jax.ShapeDtypeStruct((2, 32 * K2), F32))
    results = pl.pallas_call(
        main_kernel,
        out_shape=shapes,
        in_specs=[in_hbm] * len(operands),
        out_specs=(pl.BlockSpec(memory_space=pltpu.VMEM),) * 5,
        scratch_shapes=[vmem(tokens, F32)] * 4
        + [vmem(filters.shape, F32), vmem((1, tokens[2]), F32)]
        + [vmem(t.shape, t.dtype) for t in tables]
        + [vmem(message, F32)] * 8
        + [vmem((2 * PEERS, K2), F32)]
        + [vmem((2 * K1, 2 * K2), F32)] * 3
        + [vmem((4 * K1, 2 * K2), BF16), vmem((2 * K1, 2 * K2), F32)]
        + [vmem((2, 64, K2), F32), vmem((64, K2), F32)]
        + [
            pltpu.SemaphoreType.DMA((len(operands),)),
            pltpu.SemaphoreType.DMA((4,)),
            pltpu.SemaphoreType.DMA((4,)),
            pltpu.SemaphoreType.DMA((2,)),
        ],
        compiler_params=pltpu.CompilerParams(
            collective_id=0, has_side_effects=True, vmem_limit_bytes=40 * 1024 * 1024
        ),
        name="spectral_exchange",
    )(*[pltpu.with_memory_space_constraint(x, pltpu.HBM) for x in operands])
    return pl.pallas_call(
        store_kernel,
        out_shape=shapes,
        in_specs=[pl.BlockSpec(memory_space=pltpu.VMEM)] * 5,
        out_specs=(in_hbm,) * 5,
        scratch_shapes=[pltpu.SemaphoreType.DMA((5, 2))],
        compiler_params=pltpu.CompilerParams(vmem_limit_bytes=16 * 1024 * 1024),
        name="store",
    )(*results)


def solution(mesh):
    rows = P("batch", "seq", None)
    return jax.shard_map(
        per_device,
        mesh=mesh,
        in_specs=(rows, rows, rows, P("seq", None), P(), rows),
        out_specs=(rows, rows, rows, rows, P("seq", "batch")),
        check_vma=False,
    )
```

```python
import functools

import jax
import jax.numpy as jnp
import numpy as np
from jax import lax
from jax.experimental import pallas as pl
from jax.experimental.pallas import tpu as pltpu
from jax.sharding import PartitionSpec as P

MESH = pl.DeviceIdType.MESH
F32 = jnp.float32
BF16 = jnp.bfloat16

PEERS = 64
ROWS = 8
K1 = 128
K2 = 256
HALF = K2 // 2
FULL = K1 * K2
PART = 4


AWAY = (0, 1, 2, 1)

SHIFTS = sorted(
    ((y, z, x) for y in range(4) for z in range(2) for x in range(4) if (y, z, x) != (0, 0, 0)),
    key=lambda d: -(AWAY[d[0]] + 2 * d[1] + AWAY[d[2]]),
)


MIXED_CHUNKS = ((0,), (1,))
UP_CHUNKS = ((0, 1),)


def split_np(table):
    hi = table.astype(BF16)
    lo = (table - hi.astype(np.float64)).astype(BF16)
    return hi, lo


def rotation(angle):
    c, s = np.cos(angle), np.sin(angle)
    return np.block([[c, -s], [s, c]])


def make_tables():
    k1 = np.arange(K1)
    n1 = np.arange(PEERS)
    n2 = np.arange(K2)
    half = np.arange(HALF)
    left = rotation(2.0 * np.pi * (np.outer(n1, k1) % K1) / K1).T
    left_hi, left_lo = split_np(left)
    left_all = np.concatenate([left_hi, left_hi, left_lo], axis=1)
    left_filter = np.concatenate(
        [left_hi[:, :PEERS], left_hi[:, :PEERS], left_lo[:, :PEERS]], axis=1
    )
    inv_hi, inv_lo = split_np(left.T / FULL)
    inv = np.concatenate([inv_hi, inv_hi, inv_lo], axis=1)
    even = 2.0 * np.pi * (np.outer(half, 2 * half) % K2) / K2
    odd = 2.0 * np.pi * (np.outer(half, 2 * half + 1) % K2) / K2
    right = []
    for angle in (even, odd, odd.T):
        hi, lo = split_np(rotation(angle))
        right.append(np.concatenate([hi, hi, lo], axis=0))
    angle = 2.0 * np.pi * (np.outer(k1, n2) % FULL) / FULL
    twist = np.concatenate([np.cos(angle), np.sin(angle)], axis=0).astype(np.float32)
    return (left_all, left_filter, inv, twist, np.stack(right))


def halves(x):
    hi = x.astype(BF16)
    lo = (x - hi.astype(F32)).astype(BF16)
    return hi, lo


def dot(a, b):
    return jnp.dot(a, b, preferred_element_type=F32)


def turn_forward(section, twist):
    re, im = section[:K1], section[K1:]
    tc, ts = twist[:K1], twist[K1:]
    return re * tc + im * ts, im * tc - re * ts


def turn_inverse(re, im, twist):
    tc, ts = twist[:K1], twist[K1:]
    return re * tc - im * ts, im * tc + re * ts


def second_stage(re, im, right):
    hi, lo = halves(jnp.concatenate([re, im], axis=1))
    return dot(jnp.concatenate([hi, lo, hi], axis=1), right)


def split_stage(turned, right):
    res = jnp.concatenate([t[0] for t in turned], axis=0)
    ims = jnp.concatenate([t[1] for t in turned], axis=0)
    even = second_stage(res[:, :HALF] + res[:, HALF:], ims[:, :HALF] + ims[:, HALF:], right[0])
    odd = second_stage(res[:, :HALF] - res[:, HALF:], ims[:, :HALF] - ims[:, HALF:], right[1])
    return even, odd


def gather_rows(block_ref, row):
    return block_ref[pl.ds(row, PEERS, stride=ROWS), :]


def store_spectrum(spec_ref, channels, turned, right):
    rows = slice(channels[0] * K1, (channels[-1] + 1) * K1)
    spec_ref[rows, :K2], spec_ref[rows, K2:] = split_stage(turned, right)


def forward(block_ref, spec_ref, channels, tables):
    left_all, _, _, twist, right = tables
    turned = []
    for c in channels:
        values = [
            jnp.concatenate(
                [gather_rows(block_ref, c * 4 + b * 2), gather_rows(block_ref, c * 4 + b * 2 + 1)],
                axis=1,
            )
            for b in range(2)
        ]
        hi, lo = halves(jnp.concatenate(values, axis=0))
        section = dot(left_all[...], jnp.concatenate([hi, lo, hi], axis=0))
        turned.append(turn_forward(section, twist))
    store_spectrum(spec_ref, channels, turned, right)


def forward_filters(rows_ref, spec_ref, tables):
    _, left_filter, _, twist, right = tables
    turned = []
    for c in range(2):
        hi, lo = halves(rows_ref[c * PEERS : (c + 1) * PEERS, :])
        section = dot(left_filter[...], jnp.concatenate([hi, lo, hi], axis=0))
        turned.append(turn_forward(section, twist))
    store_spectrum(spec_ref, (0, 1), turned, right)


def multiply(left_ref, right_ref, c, parity, conjugate_left):
    rows = slice(c * K1, (c + 1) * K1)
    re = slice(parity * K2, parity * K2 + HALF)
    im = slice(parity * K2 + HALF, (parity + 1) * K2)
    lr, li = left_ref[rows, re], left_ref[rows, im]
    rr, ri = right_ref[rows, re], right_ref[rows, im]
    if conjugate_left:
        return lr * rr + li * ri, lr * ri - li * rr
    return lr * rr - li * ri, lr * ri + li * rr


def inverse(left_ref, right_ref, channels, conjugate_left, tables, real_only):
    _, _, inv, twist, right = tables
    parts = []
    for parity, k in ((0, 0), (1, 2)):
        products = [multiply(left_ref, right_ref, c, parity, conjugate_left) for c in channels]
        res = jnp.concatenate([p[0] for p in products], axis=0)
        ims = jnp.concatenate([p[1] for p in products], axis=0)
        parts.append(second_stage(ims, res, right[k]))
    even, odd = parts
    first, second = even + odd, even - odd
    results = []
    for i in range(len(channels)):
        r = slice(i * K1, (i + 1) * K1)
        im = jnp.concatenate([first[r, :HALF], second[r, :HALF]], axis=1)
        re = jnp.concatenate([first[r, HALF:], second[r, HALF:]], axis=1)
        re, im = turn_inverse(re, im, twist)
        hi, lo = halves(jnp.concatenate([re, im], axis=0))
        rows = PEERS if real_only else 2 * PEERS
        results.append(dot(inv[:rows, :], jnp.concatenate([hi, lo, hi], axis=0)))
    return results


def main_kernel(
    query_hbm, key_hbm, value_hbm, cotangent_hbm, filters_hbm, skip_hbm, *rest
):
    table_hbm, rest = rest[:5], rest[5:]
    output, query_grad, key_grad, value_grad, filter_grad = rest[:5]
    rest = rest[5:]
    query, key, value, cotangent, filters, skip = rest[:6]
    tables, rest = rest[6:11], rest[11:]
    (
        mixed_send, up_send, mixed_got, up_got, conv_send, back_send, conv_got, back_got,
        filter_rows, filter_spec, mixed_spec, up_spec, lag, lag_got,
        load_sem, send_sem, recv_sem, lag_sem,
    ) = rest
    b = lax.axis_index("batch")
    s = lax.axis_index("seq")

    loads = [
        pltpu.make_async_copy(src, dst, load_sem.at[i])
        for i, (src, dst) in enumerate(
            zip(
                (key_hbm, value_hbm, query_hbm, cotangent_hbm, filters_hbm, skip_hbm)
                + tuple(table_hbm),
                (key, value, query, cotangent, filters, skip) + tuple(tables),
            )
        )
    ]
    for load in loads:
        load.start()

    places = (
        [lax.rem(s // 16 + i, 4) * 16 for i in range(4)],
        [lax.rem(s // 8 + i, 2) * 8 for i in range(2)],
        [lax.rem(s // 2 + i, 4) * 2 for i in range(4)],
    )
    core = lax.rem(s, 2)
    own = s - core
    chips = [sum(place[i] for place, i in zip(places, shift)) for shift in SHIFTS]
    peers = [chip + i for chip in chips for i in range(2)] + [own + 1 - core]
    early = [jnp.where(own == 0, chips[0], 0)] + [jnp.where(chip == 0, chips[0], chip) for chip in chips[1:]]
    early_peers = [chip + i for chip in early for i in range(2)] + [own + 1 - core]

    barrier = pltpu.get_barrier_semaphore()
    for d in peers:
        pl.semaphore_signal(barrier, inc=1, device_id=(b, d), device_id_type=MESH)
    pl.semaphore_signal(barrier, inc=1, device_id=(1 - b, s), device_id_type=MESH)

    for first, second, left, right, target in (
        (0, 1, key, value, mixed_send),
        (2, 3, query, cotangent, up_send),
    ):
        loads[first].wait()
        loads[second].wait()
        for bb in range(2):
            for half in range(2):
                tokens = slice(half * 128, (half + 1) * 128)
                product = left[bb, tokens, :] * right[bb, tokens, :]
                target[pl.ds(bb * 2 + half, 128, stride=4), :] = product.T

    pl.semaphore_wait(barrier, PEERS)

    def block(i, channels):
        rows = len(channels) * PART
        return pl.ds(pl.multiple_of(i * ROWS + channels[0] * PART, rows), rows)

    def send(source, target, k, channels, partners):
        for d in partners:
            pltpu.make_async_remote_copy(
                src_ref=source.at[block(d, channels)],
                dst_ref=target.at[block(s, channels)],
                send_sem=send_sem.at[k, channels[0]],
                recv_sem=recv_sem.at[k, channels[0]],
                device_id=(b, d),
                device_id_type=MESH,
            ).start()
        target[block(s, channels), :] = source[block(s, channels), :]

    def settled(source, target, k, channels):
        rows = pl.ds(0, (PEERS - 1) * PART * len(channels))
        return pltpu.make_async_remote_copy(
            src_ref=source.at[rows],
            dst_ref=target.at[rows],
            send_sem=send_sem.at[k, channels[0]],
            recv_sem=recv_sem.at[k, channels[0]],
            device_id=(1 - b, s),
            device_id_type=MESH,
        )

    for channels in MIXED_CHUNKS:
        send(mixed_send, mixed_got, 0, channels, peers)
    for channels in UP_CHUNKS:
        send(up_send, up_got, 1, channels, peers)

    for load in loads[4:]:
        load.wait()
    for c in range(2):
        for n1 in range(PEERS):
            filter_rows[c * PEERS + n1 : c * PEERS + n1 + 1, :] = filters[
                c : c + 1, n1 * K2 : (n1 + 1) * K2
            ]
    forward_filters(filter_rows, filter_spec, tables)

    def spread(results, target, channels):
        for result, c in zip(results, channels):
            for bb in range(2):
                for half in range(2):
                    target[pl.ds(c * 4 + bb * 2 + half, PEERS, stride=ROWS), :] = result[
                        bb * PEERS : (bb + 1) * PEERS, half * 128 : (half + 1) * 128
                    ]

    for channels in MIXED_CHUNKS:
        settled(mixed_send, mixed_got, 0, channels).wait_recv()
        forward(mixed_got, mixed_spec, channels, tables)
        spread(inverse(mixed_spec, filter_spec, channels, False, tables, False), conv_send, channels)
        send(conv_send, conv_got, 2, channels, early_peers)
    for channels in UP_CHUNKS:
        settled(up_send, up_got, 1, channels).wait_recv()
        forward(up_got, up_spec, channels, tables)
        spread(inverse(filter_spec, up_spec, channels, True, tables, False), back_send, channels)
        send(back_send, back_got, 3, channels, early_peers)

    result = inverse(mixed_spec, up_spec, (0, 1), True, tables, True)
    for half in range(2):
        for c in range(2):
            lag[half, c * 32 : (c + 1) * 32, :] = result[c][half * 32 : (half + 1) * 32, :]
    lag_copy = pltpu.make_async_remote_copy(
        src_ref=lag.at[1 - b],
        dst_ref=lag_got,
        send_sem=lag_sem.at[0],
        recv_sem=lag_sem.at[1],
        device_id=(1 - b, s),
        device_id_type=MESH,
    )
    lag_copy.start()

    gain = skip[...]
    parts = [(bb, slice(h * 128, (h + 1) * 128), pl.ds(bb * 2 + h, 128, stride=4)) for bb in range(2) for h in range(2)]
    for channels in MIXED_CHUNKS:
        settled(conv_send, conv_got, 2, channels).wait_recv()
    for bb, tokens, rows in parts:
        hidden = conv_got[rows, :].T + gain * (key[bb, tokens, :] * value[bb, tokens, :])
        output[bb, tokens, :] = query[bb, tokens, :] * hidden
        query_grad[bb, tokens, :] = cotangent[bb, tokens, :] * hidden

    lag_copy.wait_recv()
    total = (lag[b] + lag_got[...]) * (1.0 / 128.0)
    for c in range(2):
        for n in range(32):
            filter_grad[c : c + 1, n * K2 : (n + 1) * K2] = total[c * 32 + n : c * 32 + n + 1, :]
    for channels in MIXED_CHUNKS:
        settled(mixed_send, mixed_got, 0, channels).wait_send()
        settled(conv_send, conv_got, 2, channels).wait_send()
    for channels in UP_CHUNKS:
        settled(up_send, up_got, 1, channels).wait_send()
    lag_copy.wait_send()

    for channels in UP_CHUNKS:
        settled(back_send, back_got, 3, channels).wait_recv()
    for bb, tokens, rows in parts:
        mixed_grad = back_got[rows, :].T + gain * (cotangent[bb, tokens, :] * query[bb, tokens, :])
        key_grad[bb, tokens, :] = mixed_grad * value[bb, tokens, :]
        value_grad[bb, tokens, :] = mixed_grad * key[bb, tokens, :]
    for channels in UP_CHUNKS:
        settled(back_send, back_got, 3, channels).wait_send()


def store_kernel(*refs):
    sources, targets, sem = refs[:5], refs[5:10], refs[10]
    copies = []
    for i in range(5):
        for half in range(2):
            part = (half,) if i < 4 else (slice(None), pl.ds(half * 16 * K2, 16 * K2))
            copies.append(
                pltpu.make_async_copy(sources[i].at[part], targets[i].at[part], sem.at[i, half])
            )
    for copy in copies:
        copy.start()
    for copy in copies:
        copy.wait()


def per_device(query, key, value, filters, skip, cotangent):
    tables = [jnp.asarray(t) for t in make_tables()]
    message = (PEERS * ROWS, 128)
    in_hbm = pl.BlockSpec(memory_space=pltpu.HBM)
    vmem = pltpu.VMEM
    tokens = query.shape
    operands = (query, key, value, cotangent, filters, skip.reshape(1, -1), *tables)
    block = jax.ShapeDtypeStruct(tokens, F32)
    shapes = (block, block, block, block, jax.ShapeDtypeStruct((2, 32 * K2), F32))
    results = pl.pallas_call(
        main_kernel,
        out_shape=shapes,
        in_specs=[in_hbm] * len(operands),
        out_specs=(pl.BlockSpec(memory_space=pltpu.VMEM),) * 5,
        scratch_shapes=[vmem(tokens, F32)] * 4
        + [vmem(filters.shape, F32), vmem((1, tokens[2]), F32)]
        + [vmem(t.shape, t.dtype) for t in tables]
        + [vmem(message, F32)] * 8
        + [vmem((2 * PEERS, K2), F32)]
        + [vmem((2 * K1, 2 * K2), F32)] * 3
        + [vmem((2, 64, K2), F32), vmem((64, K2), F32)]
        + [
            pltpu.SemaphoreType.DMA((len(operands),)),
            pltpu.SemaphoreType.DMA((4, 2)),
            pltpu.SemaphoreType.DMA((4, 2)),
            pltpu.SemaphoreType.DMA((2,)),
        ],
        compiler_params=pltpu.CompilerParams(
            collective_id=0, has_side_effects=True, vmem_limit_bytes=40 * 1024 * 1024
        ),
        name="spectral_exchange",
    )(*[pltpu.with_memory_space_constraint(x, pltpu.HBM) for x in operands])
    return pl.pallas_call(
        store_kernel,
        out_shape=shapes,
        in_specs=[pl.BlockSpec(memory_space=pltpu.VMEM)] * 5,
        out_specs=(in_hbm,) * 5,
        scratch_shapes=[pltpu.SemaphoreType.DMA((5, 2))],
        compiler_params=pltpu.CompilerParams(vmem_limit_bytes=16 * 1024 * 1024),
        name="store",
    )(*results)


def solution(mesh):
    rows = P("batch", "seq", None)
    return jax.shard_map(
        per_device,
        mesh=mesh,
        in_specs=(rows, rows, rows, P("seq", None), P(), rows),
        out_specs=(rows, rows, rows, rows, P("seq", "batch")),
        check_vma=False,
    )
```

```python
import functools

import jax
import jax.numpy as jnp
import numpy as np
from jax import lax
from jax.experimental import pallas as pl
from jax.experimental.pallas import tpu as pltpu
from jax.sharding import PartitionSpec as P

MESH = pl.DeviceIdType.MESH
F32 = jnp.float32
BF16 = jnp.bfloat16

PEERS = 64
ROWS = 8
K1 = 128
K2 = 256
HALF = K2 // 2
FULL = K1 * K2
PART = 4


AWAY = (0, 1, 2, 1)

SHIFTS = sorted(
    ((y, z, x) for y in range(4) for z in range(2) for x in range(4) if (y, z, x) != (0, 0, 0)),
    key=lambda d: -(AWAY[d[0]] + 2 * d[1] + AWAY[d[2]]),
)


MIXED_CHUNKS = ((0,), (1,))
UP_CHUNKS = ((0, 1),)


def split_np(table):
    hi = table.astype(BF16)
    lo = (table - hi.astype(np.float64)).astype(BF16)
    return hi, lo


def rotation(angle):
    c, s = np.cos(angle), np.sin(angle)
    return np.block([[c, -s], [s, c]])


def make_tables():
    pair = np.arange(PEERS)
    n1 = np.arange(PEERS)
    n2 = np.arange(K2)
    half = np.arange(HALF)
    angle = 2.0 * np.pi * (np.outer(pair, n1) % K1) / K1
    cosine, sine = np.cos(angle), np.sin(angle)
    alternate = np.where(n1 % 2 == 0, 1.0, -1.0)
    sine[0] = alternate
    left_hi, left_lo = split_np(np.concatenate([cosine, sine], axis=0))
    left = np.concatenate([left_hi, left_hi, left_lo], axis=1)
    sine[0] = -alternate
    inv_hi, inv_lo = split_np(np.concatenate([cosine, -sine], axis=0).T / FULL)
    inv = np.concatenate([inv_hi, inv_hi, inv_lo], axis=1)
    even = 2.0 * np.pi * (np.outer(half, 2 * half) % K2) / K2
    odd = 2.0 * np.pi * (np.outer(half, 2 * half + 1) % K2) / K2
    right = []
    for angle in (even, odd, odd.T):
        hi, lo = split_np(rotation(angle))
        right.append(np.concatenate([hi, hi, lo], axis=0))
    bins = np.concatenate([pair, [PEERS], K1 - pair[1:]])
    angle = 2.0 * np.pi * (np.outer(bins, n2) % FULL) / FULL
    twist = np.concatenate([np.cos(angle), np.sin(angle)], axis=0).astype(np.float32)
    return (left, inv, twist, np.stack(right))


def halves(x):
    hi = x.astype(BF16)
    lo = (x - hi.astype(F32)).astype(BF16)
    return hi, lo


def dot(a, b):
    return jnp.dot(a, b, preferred_element_type=F32)


def turn_forward(re, im, twist):
    tc, ts = twist[:K1], twist[K1:]
    return re * tc + im * ts, im * tc - re * ts


def turn_inverse(re, im, twist):
    tc, ts = twist[:K1], twist[K1:]
    return re * tc - im * ts, im * tc + re * ts


def second_stage(re, im, right):
    hi, lo = halves(jnp.concatenate([re, im], axis=1))
    return dot(jnp.concatenate([hi, lo, hi], axis=1), right)


def split_stage(turned, right):
    res = jnp.concatenate([t[0] for t in turned], axis=0)
    ims = jnp.concatenate([t[1] for t in turned], axis=0)
    even = second_stage(res[:, :HALF] + res[:, HALF:], ims[:, :HALF] + ims[:, HALF:], right[0])
    odd = second_stage(res[:, :HALF] - res[:, HALF:], ims[:, :HALF] - ims[:, HALF:], right[1])
    return even, odd


def gather_rows(block_ref, row):
    return block_ref[pl.ds(row, PEERS, stride=ROWS), :]


def store_spectrum(spec_ref, channels, turned, right):
    rows = slice(channels[0] * K1, (channels[-1] + 1) * K1)
    spec_ref[rows, :K2], spec_ref[rows, K2:] = split_stage(turned, right)


def first_row():
    return lax.broadcasted_iota(jnp.int32, (PEERS, K2), 0) == 0


def first_stage(left, first, second):
    hi, lo = halves(jnp.concatenate([first, second], axis=1))
    both = dot(left[...], jnp.concatenate([hi, lo, hi], axis=0))
    return both[:PEERS, :K2], both[PEERS:, :K2], both[:PEERS, K2:], both[PEERS:, K2:]


def forward(block_ref, spec_ref, channels, tables):
    left, _, twist, right = tables
    turned = []
    for c in channels:
        values = [
            jnp.concatenate(
                [gather_rows(block_ref, c * 4 + b * 2), gather_rows(block_ref, c * 4 + b * 2 + 1)],
                axis=1,
            )
            for b in range(2)
        ]
        cos0, sin0, cos1, sin1 = first_stage(left, *values)
        row = first_row()
        re = [cos0 + jnp.where(row, 0.0, sin1), jnp.where(row, sin0, cos0 - sin1)]
        im = [cos1 - jnp.where(row, 0.0, sin0), jnp.where(row, sin1, cos1 + sin0)]
        turned.append(turn_forward(jnp.concatenate(re, axis=0), jnp.concatenate(im, axis=0), twist))
    store_spectrum(spec_ref, channels, turned, right)


def forward_filters(rows_ref, spec_ref, tables):
    left, _, twist, right = tables
    cos0, sin0, cos1, sin1 = first_stage(left, rows_ref[:PEERS, :], rows_ref[PEERS:, :])
    turned = []
    for cosine, sine in ((cos0, sin0), (cos1, sin1)):
        row = first_row()
        im = jnp.where(row, 0.0, sine)
        re = jnp.concatenate([cosine, jnp.where(row, sine, cosine)], axis=0)
        turned.append(turn_forward(re, jnp.concatenate([-im, im], axis=0), twist))
    store_spectrum(spec_ref, (0, 1), turned, right)


def multiply(left_ref, right_ref, c, parity, conjugate_left):
    rows = slice(c * K1, (c + 1) * K1)
    re = slice(parity * K2, parity * K2 + HALF)
    im = slice(parity * K2 + HALF, (parity + 1) * K2)
    lr, li = left_ref[rows, re], left_ref[rows, im]
    rr, ri = right_ref[rows, re], right_ref[rows, im]
    if conjugate_left:
        return lr * rr + li * ri, lr * ri - li * rr
    return lr * rr - li * ri, lr * ri + li * rr


def inverse(left_ref, right_ref, channels, conjugate_left, tables, real_only):
    _, inv, twist, right = tables
    parts = []
    for parity, k in ((0, 0), (1, 2)):
        products = [multiply(left_ref, right_ref, c, parity, conjugate_left) for c in channels]
        res = jnp.concatenate([p[0] for p in products], axis=0)
        ims = jnp.concatenate([p[1] for p in products], axis=0)
        parts.append(second_stage(ims, res, right[k]))
    even, odd = parts
    first, second = even + odd, even - odd
    results = []
    for i in range(len(channels)):
        r = slice(i * K1, (i + 1) * K1)
        im = jnp.concatenate([first[r, :HALF], second[r, :HALF]], axis=1)
        re = jnp.concatenate([first[r, HALF:], second[r, HALF:]], axis=1)
        re, im = turn_inverse(re, im, twist)
        row = first_row()
        re_up, re_down, im_up, im_down = re[:PEERS], re[PEERS:], im[:PEERS], im[PEERS:]
        folded = jnp.concatenate(
            [
                jnp.where(row, re_up, re_up + re_down),
                jnp.where(row, re_down, im_up - im_down),
            ],
            axis=0,
        )
        if not real_only:
            other = jnp.concatenate(
                [
                    jnp.where(row, im_up, im_up + im_down),
                    jnp.where(row, im_down, re_down - re_up),
                ],
                axis=0,
            )
            folded = jnp.concatenate([folded, other], axis=1)
        hi, lo = halves(folded)
        results.append(dot(inv[...], jnp.concatenate([hi, lo, hi], axis=0)))
    return results


def main_kernel(
    query_hbm, key_hbm, value_hbm, cotangent_hbm, filters_hbm, skip_hbm, *rest
):
    table_hbm, rest = rest[:4], rest[4:]
    output, query_grad, key_grad, value_grad, filter_grad = rest[:5]
    rest = rest[5:]
    query, key, value, cotangent, filters, skip = rest[:6]
    tables, rest = rest[6:10], rest[10:]
    (
        mixed_send, up_send, mixed_got, up_got, conv_send, back_send, conv_got, back_got,
        filter_rows, filter_spec, mixed_spec, up_spec, lag, lag_got,
        load_sem, send_sem, recv_sem, lag_sem,
    ) = rest
    b = lax.axis_index("batch")
    s = lax.axis_index("seq")

    loads = [
        pltpu.make_async_copy(src, dst, load_sem.at[i])
        for i, (src, dst) in enumerate(
            zip(
                (key_hbm, value_hbm, query_hbm, cotangent_hbm, filters_hbm, skip_hbm)
                + tuple(table_hbm),
                (key, value, query, cotangent, filters, skip) + tuple(tables),
            )
        )
    ]
    for load in loads:
        load.start()

    places = (
        [lax.rem(s // 16 + i, 4) * 16 for i in range(4)],
        [lax.rem(s // 8 + i, 2) * 8 for i in range(2)],
        [lax.rem(s // 2 + i, 4) * 2 for i in range(4)],
    )
    core = lax.rem(s, 2)
    own = s - core
    chips = [sum(place[i] for place, i in zip(places, shift)) for shift in SHIFTS]
    peers = [chip + i for chip in chips for i in range(2)] + [own + 1 - core]
    early = [jnp.where(own == 0, chips[0], 0)] + [jnp.where(chip == 0, chips[0], chip) for chip in chips[1:]]
    early_peers = [chip + i for chip in early for i in range(2)] + [own + 1 - core]

    barrier = pltpu.get_barrier_semaphore()
    for d in peers:
        pl.semaphore_signal(barrier, inc=1, device_id=(b, d), device_id_type=MESH)
    pl.semaphore_signal(barrier, inc=1, device_id=(1 - b, s), device_id_type=MESH)

    for first, second, left, right, target in (
        (0, 1, key, value, mixed_send),
        (2, 3, query, cotangent, up_send),
    ):
        loads[first].wait()
        loads[second].wait()
        for bb in range(2):
            for half in range(2):
                tokens = slice(half * 128, (half + 1) * 128)
                product = left[bb, tokens, :] * right[bb, tokens, :]
                target[pl.ds(bb * 2 + half, 128, stride=4), :] = product.T

    pl.semaphore_wait(barrier, PEERS)

    def block(i, channels):
        rows = len(channels) * PART
        return pl.ds(pl.multiple_of(i * ROWS + channels[0] * PART, rows), rows)

    def send(source, target, k, channels, partners):
        for d in partners:
            pltpu.make_async_remote_copy(
                src_ref=source.at[block(d, channels)],
                dst_ref=target.at[block(s, channels)],
                send_sem=send_sem.at[k, channels[0]],
                recv_sem=recv_sem.at[k, channels[0]],
                device_id=(b, d),
                device_id_type=MESH,
            ).start()
        target[block(s, channels), :] = source[block(s, channels), :]

    def settled(source, target, k, channels):
        rows = pl.ds(0, (PEERS - 1) * PART * len(channels))
        return pltpu.make_async_remote_copy(
            src_ref=source.at[rows],
            dst_ref=target.at[rows],
            send_sem=send_sem.at[k, channels[0]],
            recv_sem=recv_sem.at[k, channels[0]],
            device_id=(1 - b, s),
            device_id_type=MESH,
        )

    for channels in MIXED_CHUNKS:
        send(mixed_send, mixed_got, 0, channels, peers)
    for channels in UP_CHUNKS:
        send(up_send, up_got, 1, channels, peers)

    for load in loads[4:]:
        load.wait()
    for c in range(2):
        for n1 in range(PEERS):
            filter_rows[c * PEERS + n1 : c * PEERS + n1 + 1, :] = filters[
                c : c + 1, n1 * K2 : (n1 + 1) * K2
            ]
    forward_filters(filter_rows, filter_spec, tables)

    def spread(results, target, channels):
        for result, c in zip(results, channels):
            for bb in range(2):
                for half in range(2):
                    lanes = slice(bb * K2 + half * 128, bb * K2 + (half + 1) * 128)
                    target[pl.ds(c * 4 + bb * 2 + half, PEERS, stride=ROWS), :] = result[:, lanes]

    for channels in MIXED_CHUNKS:
        settled(mixed_send, mixed_got, 0, channels).wait_recv()
        forward(mixed_got, mixed_spec, channels, tables)
        spread(inverse(mixed_spec, filter_spec, channels, False, tables, False), conv_send, channels)
        send(conv_send, conv_got, 2, channels, early_peers)
    for channels in UP_CHUNKS:
        settled(up_send, up_got, 1, channels).wait_recv()
        forward(up_got, up_spec, channels, tables)
        spread(inverse(filter_spec, up_spec, channels, True, tables, False), back_send, channels)
        send(back_send, back_got, 3, channels, early_peers)

    result = inverse(mixed_spec, up_spec, (0, 1), True, tables, True)
    for half in range(2):
        for c in range(2):
            lag[half, c * 32 : (c + 1) * 32, :] = result[c][half * 32 : (half + 1) * 32, :]
    lag_copy = pltpu.make_async_remote_copy(
        src_ref=lag.at[1 - b],
        dst_ref=lag_got,
        send_sem=lag_sem.at[0],
        recv_sem=lag_sem.at[1],
        device_id=(1 - b, s),
        device_id_type=MESH,
    )
    lag_copy.start()

    gain = skip[...]
    parts = [(bb, slice(h * 128, (h + 1) * 128), pl.ds(bb * 2 + h, 128, stride=4)) for bb in range(2) for h in range(2)]
    for channels in MIXED_CHUNKS:
        settled(conv_send, conv_got, 2, channels).wait_recv()
    for bb, tokens, rows in parts:
        hidden = conv_got[rows, :].T + gain * (key[bb, tokens, :] * value[bb, tokens, :])
        output[bb, tokens, :] = query[bb, tokens, :] * hidden
        query_grad[bb, tokens, :] = cotangent[bb, tokens, :] * hidden

    lag_copy.wait_recv()
    total = (lag[b] + lag_got[...]) * (1.0 / 128.0)
    for c in range(2):
        for n in range(32):
            filter_grad[c : c + 1, n * K2 : (n + 1) * K2] = total[c * 32 + n : c * 32 + n + 1, :]
    for channels in MIXED_CHUNKS:
        settled(mixed_send, mixed_got, 0, channels).wait_send()
        settled(conv_send, conv_got, 2, channels).wait_send()
    for channels in UP_CHUNKS:
        settled(up_send, up_got, 1, channels).wait_send()
    lag_copy.wait_send()

    for channels in UP_CHUNKS:
        settled(back_send, back_got, 3, channels).wait_recv()
    for bb, tokens, rows in parts:
        mixed_grad = back_got[rows, :].T + gain * (cotangent[bb, tokens, :] * query[bb, tokens, :])
        key_grad[bb, tokens, :] = mixed_grad * value[bb, tokens, :]
        value_grad[bb, tokens, :] = mixed_grad * key[bb, tokens, :]
    for channels in UP_CHUNKS:
        settled(back_send, back_got, 3, channels).wait_send()


def store_kernel(*refs):
    sources, targets, sem = refs[:5], refs[5:10], refs[10]
    copies = []
    for i in range(5):
        for half in range(2):
            part = (half,) if i < 4 else (slice(None), pl.ds(half * 16 * K2, 16 * K2))
            copies.append(
                pltpu.make_async_copy(sources[i].at[part], targets[i].at[part], sem.at[i, half])
            )
    for copy in copies:
        copy.start()
    for copy in copies:
        copy.wait()


def per_device(query, key, value, filters, skip, cotangent):
    tables = [jnp.asarray(t) for t in make_tables()]
    message = (PEERS * ROWS, 128)
    in_hbm = pl.BlockSpec(memory_space=pltpu.HBM)
    vmem = pltpu.VMEM
    tokens = query.shape
    operands = (query, key, value, cotangent, filters, skip.reshape(1, -1), *tables)
    block = jax.ShapeDtypeStruct(tokens, F32)
    shapes = (block, block, block, block, jax.ShapeDtypeStruct((2, 32 * K2), F32))
    results = pl.pallas_call(
        main_kernel,
        out_shape=shapes,
        in_specs=[in_hbm] * len(operands),
        out_specs=(pl.BlockSpec(memory_space=pltpu.VMEM),) * 5,
        scratch_shapes=[vmem(tokens, F32)] * 4
        + [vmem(filters.shape, F32), vmem((1, tokens[2]), F32)]
        + [vmem(t.shape, t.dtype) for t in tables]
        + [vmem(message, F32)] * 8
        + [vmem((2 * PEERS, K2), F32)]
        + [vmem((2 * K1, 2 * K2), F32)] * 3
        + [vmem((2, 64, K2), F32), vmem((64, K2), F32)]
        + [
            pltpu.SemaphoreType.DMA((len(operands),)),
            pltpu.SemaphoreType.DMA((4, 2)),
            pltpu.SemaphoreType.DMA((4, 2)),
            pltpu.SemaphoreType.DMA((2,)),
        ],
        compiler_params=pltpu.CompilerParams(
            collective_id=0, has_side_effects=True, vmem_limit_bytes=40 * 1024 * 1024
        ),
        name="spectral_exchange",
    )(*[pltpu.with_memory_space_constraint(x, pltpu.HBM) for x in operands])
    return pl.pallas_call(
        store_kernel,
        out_shape=shapes,
        in_specs=[pl.BlockSpec(memory_space=pltpu.VMEM)] * 5,
        out_specs=(in_hbm,) * 5,
        scratch_shapes=[pltpu.SemaphoreType.DMA((5, 2))],
        compiler_params=pltpu.CompilerParams(vmem_limit_bytes=16 * 1024 * 1024),
        name="store",
    )(*results)


def solution(mesh):
    rows = P("batch", "seq", None)
    return jax.shard_map(
        per_device,
        mesh=mesh,
        in_specs=(rows, rows, rows, P("seq", None), P(), rows),
        out_specs=(rows, rows, rows, rows, P("seq", "batch")),
        check_vma=False,
    )
```

```python
import functools

import jax
import jax.numpy as jnp
import numpy as np
from jax import lax
from jax.experimental import pallas as pl
from jax.experimental.pallas import tpu as pltpu
from jax.sharding import PartitionSpec as P

MESH = pl.DeviceIdType.MESH
F32 = jnp.float32
BF16 = jnp.bfloat16

PEERS = 64
ROWS = 8
K1 = 128
K2 = 256
HALF = K2 // 2
FULL = K1 * K2
PART = 4


AWAY = (0, 1, 2, 1)

SHIFTS = sorted(
    ((y, z, x) for y in range(4) for z in range(2) for x in range(4) if (y, z, x) != (0, 0, 0)),
    key=lambda d: -(AWAY[d[0]] + 2 * d[1] + AWAY[d[2]]),
)


MIXED_CHUNKS = ((0,), (1,))
UP_CHUNKS = ((0, 1),)


def split_np(table):
    hi = table.astype(BF16)
    lo = (table - hi.astype(np.float64)).astype(BF16)
    return hi, lo


def rotation(angle):
    c, s = np.cos(angle), np.sin(angle)
    return np.block([[c, -s], [s, c]])


def make_tables():
    pair = np.arange(PEERS)
    n1 = np.arange(PEERS)
    n2 = np.arange(K2)
    half = np.arange(HALF)
    angle = 2.0 * np.pi * (np.outer(pair, n1) % K1) / K1
    cosine, sine = np.cos(angle), np.sin(angle)
    alternate = np.where(n1 % 2 == 0, 1.0, -1.0)
    sine[0] = alternate
    left_hi, left_lo = split_np(np.concatenate([cosine, sine], axis=0))
    left = np.concatenate([left_hi, left_hi, left_lo], axis=1)
    sine[0] = -alternate
    inv_hi, inv_lo = split_np(np.concatenate([cosine, -sine], axis=0).T / FULL)
    inv = np.concatenate([inv_hi, inv_hi, inv_lo], axis=1)
    even = 2.0 * np.pi * (np.outer(half, 2 * half) % K2) / K2
    odd = 2.0 * np.pi * (np.outer(half, 2 * half + 1) % K2) / K2
    right = []
    for angle in (even, odd, odd.T):
        hi, lo = split_np(rotation(angle))
        right.append(np.concatenate([hi, hi, lo], axis=0))
    bins = np.concatenate([pair, [PEERS], K1 - pair[1:]])
    angle = 2.0 * np.pi * (np.outer(bins, n2) % FULL) / FULL
    twist = np.concatenate([np.cos(angle), np.sin(angle)], axis=0).astype(np.float32)
    return (left, inv, twist, np.stack(right))


def halves(x):
    hi = x.astype(BF16)
    lo = (x - hi.astype(F32)).astype(BF16)
    return hi, lo


def dot(a, b):
    return jnp.dot(a, b, preferred_element_type=F32)


def turn_forward(re, im, twist):
    tc, ts = twist[:K1], twist[K1:]
    return re * tc + im * ts, im * tc - re * ts


def turn_inverse(re, im, twist):
    tc, ts = twist[:K1], twist[K1:]
    return re * tc - im * ts, im * tc + re * ts


def second_stage(re, im, right):
    hi, lo = halves(jnp.concatenate([re, im], axis=1))
    return dot(jnp.concatenate([hi, lo, hi], axis=1), right)


def split_stage(turned, right):
    res = jnp.concatenate([t[0] for t in turned], axis=0)
    ims = jnp.concatenate([t[1] for t in turned], axis=0)
    even = second_stage(res[:, :HALF] + res[:, HALF:], ims[:, :HALF] + ims[:, HALF:], right[0])
    odd = second_stage(res[:, :HALF] - res[:, HALF:], ims[:, :HALF] - ims[:, HALF:], right[1])
    return even, odd


def gather_rows(block_ref, row):
    return block_ref[pl.ds(row, PEERS, stride=ROWS), :]


def store_spectrum(spec_ref, channels, turned, right):
    rows = slice(channels[0] * K1, (channels[-1] + 1) * K1)
    spec_ref[rows, :K2], spec_ref[rows, K2:] = split_stage(turned, right)


def first_row():
    return lax.broadcasted_iota(jnp.int32, (PEERS, K2), 0) == 0


def first_stage(left, first, second):
    hi, lo = halves(jnp.concatenate([first, second], axis=1))
    both = dot(left[...], jnp.concatenate([hi, lo, hi], axis=0))
    return both[:PEERS, :K2], both[PEERS:, :K2], both[:PEERS, K2:], both[PEERS:, K2:]


def forward(block_ref, spec_ref, channels, tables):
    left, _, twist, right = tables
    turned = []
    for c in channels:
        values = [
            jnp.concatenate(
                [gather_rows(block_ref, c * 4 + b * 2), gather_rows(block_ref, c * 4 + b * 2 + 1)],
                axis=1,
            )
            for b in range(2)
        ]
        cos0, sin0, cos1, sin1 = first_stage(left, *values)
        row = first_row()
        re = [cos0 + jnp.where(row, 0.0, sin1), jnp.where(row, sin0, cos0 - sin1)]
        im = [cos1 - jnp.where(row, 0.0, sin0), jnp.where(row, sin1, cos1 + sin0)]
        turned.append(turn_forward(jnp.concatenate(re, axis=0), jnp.concatenate(im, axis=0), twist))
    store_spectrum(spec_ref, channels, turned, right)


def forward_filters(rows_ref, spec_ref, tables):
    left, _, twist, right = tables
    cos0, sin0, cos1, sin1 = first_stage(left, rows_ref[:PEERS, :], rows_ref[PEERS:, :])
    turned = []
    for cosine, sine in ((cos0, sin0), (cos1, sin1)):
        row = first_row()
        im = jnp.where(row, 0.0, sine)
        re = jnp.concatenate([cosine, jnp.where(row, sine, cosine)], axis=0)
        turned.append(turn_forward(re, jnp.concatenate([-im, im], axis=0), twist))
    store_spectrum(spec_ref, (0, 1), turned, right)


def multiply(left_ref, right_ref, c, parity, conjugate_left):
    rows = slice(c * K1, (c + 1) * K1)
    re = slice(parity * K2, parity * K2 + HALF)
    im = slice(parity * K2 + HALF, (parity + 1) * K2)
    lr, li = left_ref[rows, re], left_ref[rows, im]
    rr, ri = right_ref[rows, re], right_ref[rows, im]
    if conjugate_left:
        return lr * rr + li * ri, lr * ri - li * rr
    return lr * rr - li * ri, lr * ri + li * rr


def inverse(left_ref, right_ref, channels, conjugate_left, tables, real_only):
    _, inv, twist, right = tables
    stacks = []
    for parity in range(2):
        products = [multiply(left_ref, right_ref, c, parity, conjugate_left) for c in channels]
        res = jnp.concatenate([p[0] for p in products], axis=0)
        ims = jnp.concatenate([p[1] for p in products], axis=0)
        stacks.append(halves(jnp.concatenate([ims, res], axis=1)))
    outs = []
    for i in range(len(channels)):
        r = slice(i * K1, (i + 1) * K1)
        e, o = [dot(jnp.concatenate([hi[r], lo[r], hi[r]], axis=1), right[k]) for (hi, lo), k in zip(stacks, (0, 2))]
        outs.append((e + o, e - o))
    first = jnp.concatenate([x[0] for x in outs], axis=0)
    second = jnp.concatenate([x[1] for x in outs], axis=0)
    results = []
    for i in range(len(channels)):
        r = slice(i * K1, (i + 1) * K1)
        im = jnp.concatenate([first[r, :HALF], second[r, :HALF]], axis=1)
        re = jnp.concatenate([first[r, HALF:], second[r, HALF:]], axis=1)
        re, im = turn_inverse(re, im, twist)
        row = first_row()
        re_up, re_down, im_up, im_down = re[:PEERS], re[PEERS:], im[:PEERS], im[PEERS:]
        folded = jnp.concatenate(
            [
                jnp.where(row, re_up, re_up + re_down),
                jnp.where(row, re_down, im_up - im_down),
            ],
            axis=0,
        )
        if not real_only:
            other = jnp.concatenate(
                [
                    jnp.where(row, im_up, im_up + im_down),
                    jnp.where(row, im_down, re_down - re_up),
                ],
                axis=0,
            )
            folded = jnp.concatenate([folded, other], axis=1)
        hi, lo = halves(folded)
        results.append(dot(inv[...], jnp.concatenate([hi, lo, hi], axis=0)))
    return results


def main_kernel(
    query_hbm, key_hbm, value_hbm, cotangent_hbm, filters_hbm, skip_hbm, *rest
):
    table_hbm, rest = rest[:4], rest[4:]
    output, query_grad, key_grad, value_grad, filter_grad = rest[:5]
    rest = rest[5:]
    query, key, value, cotangent, filters, skip = rest[:6]
    tables, rest = rest[6:10], rest[10:]
    (
        mixed_send, up_send, mixed_got, up_got, conv_send, back_send, conv_got, back_got,
        filter_rows, filter_spec, mixed_spec, up_spec, lag, lag_got,
        load_sem, send_sem, recv_sem, lag_sem,
    ) = rest
    b = lax.axis_index("batch")
    s = lax.axis_index("seq")

    loads = [
        pltpu.make_async_copy(src, dst, load_sem.at[i])
        for i, (src, dst) in enumerate(
            zip(
                (key_hbm, value_hbm, query_hbm, cotangent_hbm, filters_hbm, skip_hbm)
                + tuple(table_hbm),
                (key, value, query, cotangent, filters, skip) + tuple(tables),
            )
        )
    ]
    for load in loads:
        load.start()

    places = (
        [lax.rem(s // 16 + i, 4) * 16 for i in range(4)],
        [lax.rem(s // 8 + i, 2) * 8 for i in range(2)],
        [lax.rem(s // 2 + i, 4) * 2 for i in range(4)],
    )
    core = lax.rem(s, 2)
    own = s - core
    chips = [sum(place[i] for place, i in zip(places, shift)) for shift in SHIFTS]
    peers = [chip + i for chip in chips for i in range(2)] + [own + 1 - core]
    early = [jnp.where(own == 0, chips[0], 0)] + [jnp.where(chip == 0, chips[0], chip) for chip in chips[1:]]
    early_peers = [chip + i for chip in early for i in range(2)] + [own + 1 - core]

    barrier = pltpu.get_barrier_semaphore()
    for d in peers:
        pl.semaphore_signal(barrier, inc=1, device_id=(b, d), device_id_type=MESH)
    pl.semaphore_signal(barrier, inc=1, device_id=(1 - b, s), device_id_type=MESH)

    for first, second, left, right, target in (
        (0, 1, key, value, mixed_send),
        (2, 3, query, cotangent, up_send),
    ):
        loads[first].wait()
        loads[second].wait()
        for bb in range(2):
            for half in range(2):
                tokens = slice(half * 128, (half + 1) * 128)
                product = left[bb, tokens, :] * right[bb, tokens, :]
                target[pl.ds(bb * 2 + half, 128, stride=4), :] = product.T

    pl.semaphore_wait(barrier, PEERS)

    def block(i, channels):
        rows = len(channels) * PART
        return pl.ds(pl.multiple_of(i * ROWS + channels[0] * PART, rows), rows)

    def send(source, target, k, channels, partners):
        for d in partners:
            pltpu.make_async_remote_copy(
                src_ref=source.at[block(d, channels)],
                dst_ref=target.at[block(s, channels)],
                send_sem=send_sem.at[k, channels[0]],
                recv_sem=recv_sem.at[k, channels[0]],
                device_id=(b, d),
                device_id_type=MESH,
            ).start()
        target[block(s, channels), :] = source[block(s, channels), :]

    def settled(source, target, k, channels):
        rows = pl.ds(0, (PEERS - 1) * PART * len(channels))
        return pltpu.make_async_remote_copy(
            src_ref=source.at[rows],
            dst_ref=target.at[rows],
            send_sem=send_sem.at[k, channels[0]],
            recv_sem=recv_sem.at[k, channels[0]],
            device_id=(1 - b, s),
            device_id_type=MESH,
        )

    for channels in MIXED_CHUNKS:
        send(mixed_send, mixed_got, 0, channels, peers)
    for channels in UP_CHUNKS:
        send(up_send, up_got, 1, channels, peers)

    for load in loads[4:]:
        load.wait()
    for c in range(2):
        for n1 in range(PEERS):
            filter_rows[c * PEERS + n1 : c * PEERS + n1 + 1, :] = filters[
                c : c + 1, n1 * K2 : (n1 + 1) * K2
            ]
    forward_filters(filter_rows, filter_spec, tables)

    def spread(results, target, channels):
        for result, c in zip(results, channels):
            for bb in range(2):
                for half in range(2):
                    lanes = slice(bb * K2 + half * 128, bb * K2 + (half + 1) * 128)
                    target[pl.ds(c * 4 + bb * 2 + half, PEERS, stride=ROWS), :] = result[:, lanes]

    for channels in MIXED_CHUNKS:
        settled(mixed_send, mixed_got, 0, channels).wait_recv()
        forward(mixed_got, mixed_spec, channels, tables)
        spread(inverse(mixed_spec, filter_spec, channels, False, tables, False), conv_send, channels)
        send(conv_send, conv_got, 2, channels, peers)
    for channels in UP_CHUNKS:
        settled(up_send, up_got, 1, channels).wait_recv()
        forward(up_got, up_spec, channels, tables)
        spread(inverse(filter_spec, up_spec, channels, True, tables, False), back_send, channels)
        send(back_send, back_got, 3, channels, early_peers)

    result = inverse(mixed_spec, up_spec, (0, 1), True, tables, True)
    for half in range(2):
        for c in range(2):
            lag[half, c * 32 : (c + 1) * 32, :] = result[c][half * 32 : (half + 1) * 32, :]
    lag_copy = pltpu.make_async_remote_copy(
        src_ref=lag.at[1 - b],
        dst_ref=lag_got,
        send_sem=lag_sem.at[0],
        recv_sem=lag_sem.at[1],
        device_id=(1 - b, s),
        device_id_type=MESH,
    )
    lag_copy.start()

    gain = skip[...]
    parts = [(bb, slice(h * 128, (h + 1) * 128), pl.ds(bb * 2 + h, 128, stride=4)) for bb in range(2) for h in range(2)]
    for channels in MIXED_CHUNKS:
        settled(conv_send, conv_got, 2, channels).wait_recv()
    for bb, tokens, rows in parts:
        hidden = conv_got[rows, :].T + gain * (key[bb, tokens, :] * value[bb, tokens, :])
        output[bb, tokens, :] = query[bb, tokens, :] * hidden
        query_grad[bb, tokens, :] = cotangent[bb, tokens, :] * hidden

    lag_copy.wait_recv()
    total = (lag[b] + lag_got[...]) * (1.0 / 128.0)
    for c in range(2):
        for n in range(32):
            filter_grad[c : c + 1, n * K2 : (n + 1) * K2] = total[c * 32 + n : c * 32 + n + 1, :]
    for channels in MIXED_CHUNKS:
        settled(mixed_send, mixed_got, 0, channels).wait_send()
        settled(conv_send, conv_got, 2, channels).wait_send()
    for channels in UP_CHUNKS:
        settled(up_send, up_got, 1, channels).wait_send()
    lag_copy.wait_send()

    for channels in UP_CHUNKS:
        settled(back_send, back_got, 3, channels).wait_recv()
    for bb, tokens, rows in parts:
        mixed_grad = back_got[rows, :].T + gain * (cotangent[bb, tokens, :] * query[bb, tokens, :])
        key_grad[bb, tokens, :] = mixed_grad * value[bb, tokens, :]
        value_grad[bb, tokens, :] = mixed_grad * key[bb, tokens, :]
    for channels in UP_CHUNKS:
        settled(back_send, back_got, 3, channels).wait_send()


def store_kernel(*refs):
    sources, targets, sem = refs[:5], refs[5:10], refs[10]
    copies = []
    for i in range(5):
        for half in range(2):
            part = (half,) if i < 4 else (slice(None), pl.ds(half * 16 * K2, 16 * K2))
            copies.append(
                pltpu.make_async_copy(sources[i].at[part], targets[i].at[part], sem.at[i, half])
            )
    for copy in copies:
        copy.start()
    for copy in copies:
        copy.wait()


def per_device(query, key, value, filters, skip, cotangent):
    tables = [jnp.asarray(t) for t in make_tables()]
    message = (PEERS * ROWS, 128)
    in_hbm = pl.BlockSpec(memory_space=pltpu.HBM)
    vmem = pltpu.VMEM
    tokens = query.shape
    operands = (query, key, value, cotangent, filters, skip.reshape(1, -1), *tables)
    block = jax.ShapeDtypeStruct(tokens, F32)
    shapes = (block, block, block, block, jax.ShapeDtypeStruct((2, 32 * K2), F32))
    results = pl.pallas_call(
        main_kernel,
        out_shape=shapes,
        in_specs=[in_hbm] * len(operands),
        out_specs=(pl.BlockSpec(memory_space=pltpu.VMEM),) * 5,
        scratch_shapes=[vmem(tokens, F32)] * 4
        + [vmem(filters.shape, F32), vmem((1, tokens[2]), F32)]
        + [vmem(t.shape, t.dtype) for t in tables]
        + [vmem(message, F32)] * 8
        + [vmem((2 * PEERS, K2), F32)]
        + [vmem((2 * K1, 2 * K2), F32)] * 3
        + [vmem((2, 64, K2), F32), vmem((64, K2), F32)]
        + [
            pltpu.SemaphoreType.DMA((len(operands),)),
            pltpu.SemaphoreType.DMA((4, 2)),
            pltpu.SemaphoreType.DMA((4, 2)),
            pltpu.SemaphoreType.DMA((2,)),
        ],
        compiler_params=pltpu.CompilerParams(
            collective_id=0, has_side_effects=True, vmem_limit_bytes=40 * 1024 * 1024
        ),
        name="spectral_exchange",
    )(*[pltpu.with_memory_space_constraint(x, pltpu.HBM) for x in operands])
    return pl.pallas_call(
        store_kernel,
        out_shape=shapes,
        in_specs=[pl.BlockSpec(memory_space=pltpu.VMEM)] * 5,
        out_specs=(in_hbm,) * 5,
        scratch_shapes=[pltpu.SemaphoreType.DMA((5, 2))],
        compiler_params=pltpu.CompilerParams(vmem_limit_bytes=16 * 1024 * 1024),
        name="store",
    )(*results)


def solution(mesh):
    rows = P("batch", "seq", None)
    return jax.shard_map(
        per_device,
        mesh=mesh,
        in_specs=(rows, rows, rows, P("seq", None), P(), rows),
        out_specs=(rows, rows, rows, rows, P("seq", "batch")),
        check_vma=False,
    )
```

```python
import functools

import jax
import jax.numpy as jnp
import numpy as np
from jax import lax
from jax.experimental import pallas as pl
from jax.experimental.pallas import tpu as pltpu
from jax.sharding import PartitionSpec as P

MESH = pl.DeviceIdType.MESH
F32 = jnp.float32
BF16 = jnp.bfloat16

PEERS = 64
ROWS = 8
K1 = 128
K2 = 256
HALF = K2 // 2
FULL = K1 * K2
PART = 4


AWAY = (0, 1, 2, 1)

SHIFTS = sorted(
    ((y, z, x) for y in range(4) for z in range(2) for x in range(4) if (y, z, x) != (0, 0, 0)),
    key=lambda d: -(AWAY[d[0]] + 2 * d[1] + AWAY[d[2]]),
)


MIXED_CHUNKS = ((0,), (1,))
UP_CHUNKS = ((0, 1),)


def split_np(table):
    hi = table.astype(BF16)
    lo = (table - hi.astype(np.float64)).astype(BF16)
    return hi, lo


def rotation(angle):
    c, s = np.cos(angle), np.sin(angle)
    return np.block([[c, -s], [s, c]])


def make_tables():
    pair = np.arange(PEERS)
    n1 = np.arange(PEERS)
    n2 = np.arange(K2)
    half = np.arange(HALF)
    angle = 2.0 * np.pi * (np.outer(pair, n1) % K1) / K1
    cosine, sine = np.cos(angle), np.sin(angle)
    alternate = np.where(n1 % 2 == 0, 1.0, -1.0)
    sine[0] = alternate
    left_hi, left_lo = split_np(np.concatenate([cosine, sine], axis=0))
    left = np.concatenate([left_hi, left_hi, left_lo], axis=1)
    sine[0] = -alternate
    inv_hi, inv_lo = split_np(np.concatenate([cosine, -sine], axis=0).T / FULL)
    inv = np.concatenate([inv_hi, inv_hi, inv_lo], axis=1)
    even = 2.0 * np.pi * (np.outer(half, 2 * half) % K2) / K2
    odd = 2.0 * np.pi * (np.outer(half, 2 * half + 1) % K2) / K2
    right = []
    for angle in (even, odd, odd.T):
        hi, lo = split_np(rotation(angle))
        right.append(np.concatenate([hi, hi, lo], axis=0))
    bins = np.concatenate([pair, [PEERS], K1 - pair[1:]])
    angle = 2.0 * np.pi * (np.outer(bins, n2) % FULL) / FULL
    twist = np.concatenate([np.cos(angle), np.sin(angle)], axis=0).astype(np.float32)
    return (left, inv, twist, np.stack(right))


def halves(x):
    hi = x.astype(BF16)
    lo = (x - hi.astype(F32)).astype(BF16)
    return hi, lo


def dot(a, b):
    return jnp.dot(a, b, preferred_element_type=F32)


def turn_forward(re, im, twist):
    tc, ts = twist[:K1], twist[K1:]
    return re * tc + im * ts, im * tc - re * ts


def turn_inverse(re, im, twist):
    tc, ts = twist[:K1], twist[K1:]
    return re * tc - im * ts, im * tc + re * ts


def second_stage(re, im, right):
    hi, lo = halves(jnp.concatenate([re, im], axis=1))
    return dot(jnp.concatenate([hi, lo, hi], axis=1), right)


def split_stage(turned, right):
    res = jnp.concatenate([t[0] for t in turned], axis=0)
    ims = jnp.concatenate([t[1] for t in turned], axis=0)
    even = second_stage(res[:, :HALF] + res[:, HALF:], ims[:, :HALF] + ims[:, HALF:], right[0])
    odd = second_stage(res[:, :HALF] - res[:, HALF:], ims[:, :HALF] - ims[:, HALF:], right[1])
    return even, odd


def gather_rows(block_ref, row):
    return block_ref[pl.ds(row, PEERS, stride=ROWS), :]


def store_spectrum(spec_ref, channels, turned, right):
    rows = slice(channels[0] * K1, (channels[-1] + 1) * K1)
    spec_ref[rows, :K2], spec_ref[rows, K2:] = split_stage(turned, right)


def first_row():
    return lax.broadcasted_iota(jnp.int32, (PEERS, K2), 0) == 0


def first_stage(left, first, second):
    hi, lo = halves(jnp.concatenate([first, second], axis=1))
    both = dot(left[...], jnp.concatenate([hi, lo, hi], axis=0))
    return both[:PEERS, :K2], both[PEERS:, :K2], both[:PEERS, K2:], both[PEERS:, K2:]


def forward(block_ref, spec_ref, channels, tables):
    left, _, twist, right = tables
    turned = []
    for c in channels:
        values = [
            jnp.concatenate(
                [gather_rows(block_ref, c * 4 + b * 2), gather_rows(block_ref, c * 4 + b * 2 + 1)],
                axis=1,
            )
            for b in range(2)
        ]
        cos0, sin0, cos1, sin1 = first_stage(left, *values)
        row = first_row()
        re = [cos0 + jnp.where(row, 0.0, sin1), jnp.where(row, sin0, cos0 - sin1)]
        im = [cos1 - jnp.where(row, 0.0, sin0), jnp.where(row, sin1, cos1 + sin0)]
        turned.append(turn_forward(jnp.concatenate(re, axis=0), jnp.concatenate(im, axis=0), twist))
    store_spectrum(spec_ref, channels, turned, right)


def forward_filters(rows_ref, spec_ref, tables):
    left, _, twist, right = tables
    cos0, sin0, cos1, sin1 = first_stage(left, rows_ref[:PEERS, :], rows_ref[PEERS:, :])
    turned = []
    for cosine, sine in ((cos0, sin0), (cos1, sin1)):
        row = first_row()
        im = jnp.where(row, 0.0, sine)
        re = jnp.concatenate([cosine, jnp.where(row, sine, cosine)], axis=0)
        turned.append(turn_forward(re, jnp.concatenate([-im, im], axis=0), twist))
    store_spectrum(spec_ref, (0, 1), turned, right)


def multiply(left_ref, right_ref, c, parity, conjugate_left):
    rows = slice(c * K1, (c + 1) * K1)
    re = slice(parity * K2, parity * K2 + HALF)
    im = slice(parity * K2 + HALF, (parity + 1) * K2)
    lr, li = left_ref[rows, re], left_ref[rows, im]
    rr, ri = right_ref[rows, re], right_ref[rows, im]
    if conjugate_left:
        return lr * rr + li * ri, lr * ri - li * rr
    return lr * rr - li * ri, lr * ri + li * rr


def inverse(left_ref, right_ref, channels, conjugate_left, tables, real_only):
    _, inv, twist, right = tables
    stacks = []
    for parity in range(2):
        products = [multiply(left_ref, right_ref, c, parity, conjugate_left) for c in channels]
        res = jnp.concatenate([p[0] for p in products], axis=0)
        ims = jnp.concatenate([p[1] for p in products], axis=0)
        stacks.append(halves(jnp.concatenate([ims, res], axis=1)))
    outs = []
    for i in range(len(channels)):
        r = slice(i * K1, (i + 1) * K1)
        e, o = [dot(jnp.concatenate([hi[r], lo[r], hi[r]], axis=1), right[k]) for (hi, lo), k in zip(stacks, (0, 2))]
        outs.append((e + o, e - o))
    first = jnp.concatenate([x[0] for x in outs], axis=0)
    second = jnp.concatenate([x[1] for x in outs], axis=0)
    results = []
    for i in range(len(channels)):
        r = slice(i * K1, (i + 1) * K1)
        im = jnp.concatenate([first[r, :HALF], second[r, :HALF]], axis=1)
        re = jnp.concatenate([first[r, HALF:], second[r, HALF:]], axis=1)
        re, im = turn_inverse(re, im, twist)
        row = first_row()
        re_up, re_down, im_up, im_down = re[:PEERS], re[PEERS:], im[:PEERS], im[PEERS:]
        folded = jnp.concatenate(
            [
                jnp.where(row, re_up, re_up + re_down),
                jnp.where(row, re_down, im_up - im_down),
            ],
            axis=0,
        )
        if not real_only:
            other = jnp.concatenate(
                [
                    jnp.where(row, im_up, im_up + im_down),
                    jnp.where(row, im_down, re_down - re_up),
                ],
                axis=0,
            )
            folded = jnp.concatenate([folded, other], axis=1)
        hi, lo = halves(folded)
        results.append(dot(inv[...], jnp.concatenate([hi, lo, hi], axis=0)))
    return results


def main_kernel(
    query_hbm, key_hbm, value_hbm, cotangent_hbm, filters_hbm, skip_hbm, *rest
):
    table_hbm, rest = rest[:4], rest[4:]
    output, query_grad, key_grad, value_grad, filter_grad = rest[:5]
    rest = rest[5:]
    query, key, value, cotangent, filters, skip = rest[:6]
    tables, rest = rest[6:10], rest[10:]
    (
        mixed_send, up_send, mixed_got, up_got, conv_send, back_send, conv_got, back_got,
        filter_rows, filter_spec, mixed_spec, up_spec, lag, lag_got,
        load_sem, send_sem, recv_sem, lag_sem,
    ) = rest
    b = lax.axis_index("batch")
    s = lax.axis_index("seq")

    loads = [
        pltpu.make_async_copy(src, dst, load_sem.at[i])
        for i, (src, dst) in enumerate(
            zip(
                (key_hbm, value_hbm, query_hbm, cotangent_hbm, filters_hbm, skip_hbm)
                + tuple(table_hbm),
                (key, value, query, cotangent, filters, skip) + tuple(tables),
            )
        )
    ]
    for load in loads:
        load.start()

    places = (
        [lax.rem(s // 16 + i, 4) * 16 for i in range(4)],
        [lax.rem(s // 8 + i, 2) * 8 for i in range(2)],
        [lax.rem(s // 2 + i, 4) * 2 for i in range(4)],
    )
    core = lax.rem(s, 2)
    own = s - core
    chips = [sum(place[i] for place, i in zip(places, shift)) for shift in SHIFTS]
    peers = [chip + i for chip in chips for i in range(2)] + [own + 1 - core]
    early = [jnp.where(own == 0, chips[0], 0)] + [jnp.where(chip == 0, chips[0], chip) for chip in chips[1:]]
    early_peers = [chip + i for chip in early for i in range(2)] + [own + 1 - core]

    barrier = pltpu.get_barrier_semaphore()
    for d in peers:
        pl.semaphore_signal(barrier, inc=1, device_id=(b, d), device_id_type=MESH)
    pl.semaphore_signal(barrier, inc=1, device_id=(1 - b, s), device_id_type=MESH)

    for first, second, left, right, target in (
        (0, 1, key, value, mixed_send),
        (2, 3, query, cotangent, up_send),
    ):
        loads[first].wait()
        loads[second].wait()
        for bb in range(2):
            for half in range(2):
                tokens = slice(half * 128, (half + 1) * 128)
                product = left[bb, tokens, :] * right[bb, tokens, :]
                target[pl.ds(bb * 2 + half, 128, stride=4), :] = product.T

    pl.semaphore_wait(barrier, PEERS)

    def block(i, channels):
        rows = len(channels) * PART
        return pl.ds(pl.multiple_of(i * ROWS + channels[0] * PART, rows), rows)

    def send(source, target, k, channels, partners, keep=True):
        for d in partners:
            pltpu.make_async_remote_copy(
                src_ref=source.at[block(d, channels)],
                dst_ref=target.at[block(s, channels)],
                send_sem=send_sem.at[k, channels[0]],
                recv_sem=recv_sem.at[k, channels[0]],
                device_id=(b, d),
                device_id_type=MESH,
            ).start()
        if keep:
            target[block(s, channels), :] = source[block(s, channels), :]

    def settled(source, target, k, channels):
        rows = pl.ds(0, (PEERS - 1) * PART * len(channels))
        return pltpu.make_async_remote_copy(
            src_ref=source.at[rows],
            dst_ref=target.at[rows],
            send_sem=send_sem.at[k, channels[0]],
            recv_sem=recv_sem.at[k, channels[0]],
            device_id=(1 - b, s),
            device_id_type=MESH,
        )

    for channels in MIXED_CHUNKS:
        send(mixed_send, mixed_got, 0, channels, peers)
    for channels in UP_CHUNKS:
        send(up_send, up_got, 1, channels, peers)

    for load in loads[4:]:
        load.wait()
    for c in range(2):
        for n1 in range(PEERS):
            filter_rows[c * PEERS + n1 : c * PEERS + n1 + 1, :] = filters[
                c : c + 1, n1 * K2 : (n1 + 1) * K2
            ]
    forward_filters(filter_rows, filter_spec, tables)

    def spread(results, target, channels):
        for result, c in zip(results, channels):
            for bb in range(2):
                for half in range(2):
                    lanes = slice(bb * K2 + half * 128, bb * K2 + (half + 1) * 128)
                    target[pl.ds(c * 4 + bb * 2 + half, PEERS, stride=ROWS), :] = result[:, lanes]

    for channels in MIXED_CHUNKS:
        settled(mixed_send, mixed_got, 0, channels).wait_recv()
        forward(mixed_got, mixed_spec, channels, tables)
        spread(inverse(mixed_spec, filter_spec, channels, False, tables, False), conv_send, channels)
        send(conv_send, conv_got, 2, channels, peers)
    both = (0, 1)
    settled(up_send, up_got, 1, both).wait_recv()
    forward(up_got, up_spec, both, tables)
    spread(inverse(filter_spec, up_spec, both, True, tables, False), back_send, both)
    send(back_send, back_got, 3, both, early_peers[:2], False)

    result = inverse(mixed_spec, up_spec, (0, 1), True, tables, True)
    for half in range(2):
        for c in range(2):
            lag[half, c * 32 : (c + 1) * 32, :] = result[c][half * 32 : (half + 1) * 32, :]
    lag_copy = pltpu.make_async_remote_copy(
        src_ref=lag.at[1 - b],
        dst_ref=lag_got,
        send_sem=lag_sem.at[0],
        recv_sem=lag_sem.at[1],
        device_id=(1 - b, s),
        device_id_type=MESH,
    )
    lag_copy.start()
    send(back_send, back_got, 3, both, early_peers[2:])

    gain = skip[...]
    parts = [(bb, slice(h * 128, (h + 1) * 128), pl.ds(bb * 2 + h, 128, stride=4)) for bb in range(2) for h in range(2)]
    for channels in MIXED_CHUNKS:
        settled(conv_send, conv_got, 2, channels).wait_recv()
    for bb, tokens, rows in parts:
        hidden = conv_got[rows, :].T + gain * (key[bb, tokens, :] * value[bb, tokens, :])
        output[bb, tokens, :] = query[bb, tokens, :] * hidden
        query_grad[bb, tokens, :] = cotangent[bb, tokens, :] * hidden

    lag_copy.wait_recv()
    total = (lag[b] + lag_got[...]) * (1.0 / 128.0)
    for c in range(2):
        for n in range(32):
            filter_grad[c : c + 1, n * K2 : (n + 1) * K2] = total[c * 32 + n : c * 32 + n + 1, :]
    for channels in MIXED_CHUNKS:
        settled(mixed_send, mixed_got, 0, channels).wait_send()
        settled(conv_send, conv_got, 2, channels).wait_send()
    for channels in UP_CHUNKS:
        settled(up_send, up_got, 1, channels).wait_send()
    lag_copy.wait_send()

    for channels in UP_CHUNKS:
        settled(back_send, back_got, 3, channels).wait_recv()
    for bb, tokens, rows in parts:
        mixed_grad = back_got[rows, :].T + gain * (cotangent[bb, tokens, :] * query[bb, tokens, :])
        key_grad[bb, tokens, :] = mixed_grad * value[bb, tokens, :]
        value_grad[bb, tokens, :] = mixed_grad * key[bb, tokens, :]
    for channels in UP_CHUNKS:
        settled(back_send, back_got, 3, channels).wait_send()


def store_kernel(*refs):
    sources, targets, sem = refs[:5], refs[5:10], refs[10]
    copies = []
    for i in range(5):
        for half in range(2):
            part = (half,) if i < 4 else (slice(None), pl.ds(half * 16 * K2, 16 * K2))
            copies.append(
                pltpu.make_async_copy(sources[i].at[part], targets[i].at[part], sem.at[i, half])
            )
    for copy in copies:
        copy.start()
    for copy in copies:
        copy.wait()


def per_device(query, key, value, filters, skip, cotangent):
    tables = [jnp.asarray(t) for t in make_tables()]
    message = (PEERS * ROWS, 128)
    in_hbm = pl.BlockSpec(memory_space=pltpu.HBM)
    vmem = pltpu.VMEM
    tokens = query.shape
    operands = (query, key, value, cotangent, filters, skip.reshape(1, -1), *tables)
    block = jax.ShapeDtypeStruct(tokens, F32)
    shapes = (block, block, block, block, jax.ShapeDtypeStruct((2, 32 * K2), F32))
    results = pl.pallas_call(
        main_kernel,
        out_shape=shapes,
        in_specs=[in_hbm] * len(operands),
        out_specs=(pl.BlockSpec(memory_space=pltpu.VMEM),) * 5,
        scratch_shapes=[vmem(tokens, F32)] * 4
        + [vmem(filters.shape, F32), vmem((1, tokens[2]), F32)]
        + [vmem(t.shape, t.dtype) for t in tables]
        + [vmem(message, F32)] * 8
        + [vmem((2 * PEERS, K2), F32)]
        + [vmem((2 * K1, 2 * K2), F32)] * 3
        + [vmem((2, 64, K2), F32), vmem((64, K2), F32)]
        + [
            pltpu.SemaphoreType.DMA((len(operands),)),
            pltpu.SemaphoreType.DMA((4, 2)),
            pltpu.SemaphoreType.DMA((4, 2)),
            pltpu.SemaphoreType.DMA((2,)),
        ],
        compiler_params=pltpu.CompilerParams(
            collective_id=0, has_side_effects=True, vmem_limit_bytes=40 * 1024 * 1024
        ),
        name="spectral_exchange",
    )(*[pltpu.with_memory_space_constraint(x, pltpu.HBM) for x in operands])
    return pl.pallas_call(
        store_kernel,
        out_shape=shapes,
        in_specs=[pl.BlockSpec(memory_space=pltpu.VMEM)] * 5,
        out_specs=(in_hbm,) * 5,
        scratch_shapes=[pltpu.SemaphoreType.DMA((5, 2))],
        compiler_params=pltpu.CompilerParams(vmem_limit_bytes=16 * 1024 * 1024),
        name="store",
    )(*results)


def solution(mesh):
    rows = P("batch", "seq", None)
    return jax.shard_map(
        per_device,
        mesh=mesh,
        in_specs=(rows, rows, rows, P("seq", None), P(), rows),
        out_specs=(rows, rows, rows, rows, P("seq", "batch")),
        check_vma=False,
    )
```

```python
import functools

import jax
import jax.numpy as jnp
import numpy as np
from jax import lax
from jax.experimental import pallas as pl
from jax.experimental.pallas import tpu as pltpu
from jax.sharding import PartitionSpec as P

MESH = pl.DeviceIdType.MESH
F32 = jnp.float32
BF16 = jnp.bfloat16

PEERS = 64
ROWS = 8
K1 = 128
K2 = 256
HALF = K2 // 2
FULL = K1 * K2
PART = 4


AWAY = (0, 1, 2, 1)

SHIFTS = sorted(
    ((y, z, x) for y in range(4) for z in range(2) for x in range(4) if (y, z, x) != (0, 0, 0)),
    key=lambda d: -(AWAY[d[0]] + 2 * d[1] + AWAY[d[2]]),
)


MIXED_CHUNKS = ((0,), (1,))
UP_CHUNKS = ((0, 1),)


def split_np(table):
    hi = table.astype(BF16)
    lo = (table - hi.astype(np.float64)).astype(BF16)
    return hi, lo


def rotation(angle):
    c, s = np.cos(angle), np.sin(angle)
    return np.block([[c, -s], [s, c]])


def make_tables():
    pair = np.arange(PEERS)
    n1 = np.arange(PEERS)
    n2 = np.arange(K2)
    half = np.arange(HALF)
    angle = 2.0 * np.pi * (np.outer(pair, n1) % K1) / K1
    cosine, sine = np.cos(angle), np.sin(angle)
    alternate = np.where(n1 % 2 == 0, 1.0, -1.0)
    sine[0] = alternate
    left_hi, left_lo = split_np(np.concatenate([cosine, sine], axis=0))
    left = np.concatenate([left_hi, left_hi, left_lo], axis=1)
    sine[0] = -alternate
    inv_hi, inv_lo = split_np(np.concatenate([cosine, -sine], axis=0).T / FULL)
    inv = np.concatenate([inv_hi, inv_hi, inv_lo], axis=1)
    even = 2.0 * np.pi * (np.outer(half, 2 * half) % K2) / K2
    odd = 2.0 * np.pi * (np.outer(half, 2 * half + 1) % K2) / K2
    right = []
    for angle in (even, odd, odd.T):
        hi, lo = split_np(rotation(angle))
        right.append(np.concatenate([hi, hi, lo], axis=0))
    bins = np.concatenate([pair, [PEERS], K1 - pair[1:]])
    angle = 2.0 * np.pi * (np.outer(bins, n2) % FULL) / FULL
    twist = np.concatenate([np.cos(angle), np.sin(angle)], axis=0).astype(np.float32)
    return (left, inv, twist, np.stack(right))


def halves(x):
    hi = x.astype(BF16)
    lo = (x - hi.astype(F32)).astype(BF16)
    return hi, lo


def dot(a, b):
    return jnp.dot(a, b, preferred_element_type=F32)


def turn_forward(re, im, twist):
    tc, ts = twist[:K1], twist[K1:]
    return re * tc + im * ts, im * tc - re * ts


def turn_inverse(re, im, twist):
    tc, ts = twist[:K1], twist[K1:]
    return re * tc - im * ts, im * tc + re * ts


def second_stage(re, im, right):
    hi, lo = halves(jnp.concatenate([re, im], axis=1))
    return dot(jnp.concatenate([hi, lo, hi], axis=1), right)


def split_stage(turned, right):
    res = jnp.concatenate([t[0] for t in turned], axis=0)
    ims = jnp.concatenate([t[1] for t in turned], axis=0)
    even = second_stage(res[:, :HALF] + res[:, HALF:], ims[:, :HALF] + ims[:, HALF:], right[0])
    odd = second_stage(res[:, :HALF] - res[:, HALF:], ims[:, :HALF] - ims[:, HALF:], right[1])
    return even, odd


def gather_rows(block_ref, row):
    return block_ref[pl.ds(row, PEERS, stride=ROWS), :]


def store_spectrum(spec_ref, channels, turned, right):
    rows = slice(channels[0] * K1, (channels[-1] + 1) * K1)
    spec_ref[rows, :K2], spec_ref[rows, K2:] = split_stage(turned, right)


def first_row():
    return lax.broadcasted_iota(jnp.int32, (PEERS, K2), 0) == 0


def first_stage(left, first, second):
    hi, lo = halves(jnp.concatenate([first, second], axis=1))
    both = dot(left[...], jnp.concatenate([hi, lo, hi], axis=0))
    return both[:PEERS, :K2], both[PEERS:, :K2], both[:PEERS, K2:], both[PEERS:, K2:]


def forward(block_ref, spec_ref, channels, tables):
    left, _, twist, right = tables
    turned = []
    for c in channels:
        values = [
            jnp.concatenate(
                [gather_rows(block_ref, c * 4 + b * 2), gather_rows(block_ref, c * 4 + b * 2 + 1)],
                axis=1,
            )
            for b in range(2)
        ]
        cos0, sin0, cos1, sin1 = first_stage(left, *values)
        row = first_row()
        re = [cos0 + jnp.where(row, 0.0, sin1), jnp.where(row, sin0, cos0 - sin1)]
        im = [cos1 - jnp.where(row, 0.0, sin0), jnp.where(row, sin1, cos1 + sin0)]
        turned.append(turn_forward(jnp.concatenate(re, axis=0), jnp.concatenate(im, axis=0), twist))
    store_spectrum(spec_ref, channels, turned, right)


def forward_filters(rows_ref, spec_ref, tables):
    left, _, twist, right = tables
    cos0, sin0, cos1, sin1 = first_stage(left, rows_ref[:PEERS, :], rows_ref[PEERS:, :])
    turned = []
    for cosine, sine in ((cos0, sin0), (cos1, sin1)):
        row = first_row()
        im = jnp.where(row, 0.0, sine)
        re = jnp.concatenate([cosine, jnp.where(row, sine, cosine)], axis=0)
        turned.append(turn_forward(re, jnp.concatenate([-im, im], axis=0), twist))
    store_spectrum(spec_ref, (0, 1), turned, right)


def multiply(left_ref, right_ref, c, parity, conjugate_left):
    rows = slice(c * K1, (c + 1) * K1)
    re = slice(parity * K2, parity * K2 + HALF)
    im = slice(parity * K2 + HALF, (parity + 1) * K2)
    lr, li = left_ref[rows, re], left_ref[rows, im]
    rr, ri = right_ref[rows, re], right_ref[rows, im]
    if conjugate_left:
        return lr * rr + li * ri, lr * ri - li * rr
    return lr * rr - li * ri, lr * ri + li * rr


def inverse(left_ref, right_ref, channels, conjugate_left, tables, real_only):
    _, inv, twist, right = tables
    stacks = []
    for parity in range(2):
        products = [multiply(left_ref, right_ref, c, parity, conjugate_left) for c in channels]
        res = jnp.concatenate([p[0] for p in products], axis=0)
        ims = jnp.concatenate([p[1] for p in products], axis=0)
        stacks.append(halves(jnp.concatenate([ims, res], axis=1)))
    outs = []
    for i in range(len(channels)):
        r = slice(i * K1, (i + 1) * K1)
        e, o = [dot(jnp.concatenate([hi[r], lo[r], hi[r]], axis=1), right[k]) for (hi, lo), k in zip(stacks, (0, 2))]
        outs.append((e + o, e - o))
    first = jnp.concatenate([x[0] for x in outs], axis=0)
    second = jnp.concatenate([x[1] for x in outs], axis=0)
    results = []
    for i in range(len(channels)):
        r = slice(i * K1, (i + 1) * K1)
        im = jnp.concatenate([first[r, :HALF], second[r, :HALF]], axis=1)
        re = jnp.concatenate([first[r, HALF:], second[r, HALF:]], axis=1)
        re, im = turn_inverse(re, im, twist)
        row = first_row()
        re_up, re_down, im_up, im_down = re[:PEERS], re[PEERS:], im[:PEERS], im[PEERS:]
        folded = jnp.concatenate(
            [
                jnp.where(row, re_up, re_up + re_down),
                jnp.where(row, re_down, im_up - im_down),
            ],
            axis=0,
        )
        if not real_only:
            other = jnp.concatenate(
                [
                    jnp.where(row, im_up, im_up + im_down),
                    jnp.where(row, im_down, re_down - re_up),
                ],
                axis=0,
            )
            folded = jnp.concatenate([folded, other], axis=1)
        hi, lo = halves(folded)
        results.append(dot(inv[...], jnp.concatenate([hi, lo, hi], axis=0)))
    return results


def main_kernel(
    query_hbm, key_hbm, value_hbm, cotangent_hbm, filters_hbm, skip_hbm, *rest
):
    table_hbm, rest = rest[:4], rest[4:]
    output, query_grad, key_grad, value_grad, filter_grad = rest[:5]
    rest = rest[5:]
    query, key, value, cotangent, filters, skip = rest[:6]
    tables, rest = rest[6:10], rest[10:]
    (
        mixed_send, up_send, mixed_got, up_got, conv_send, back_send, conv_got, back_got,
        filter_rows, filter_spec, mixed_spec, up_spec, lag, lag_got,
        load_sem, send_sem, recv_sem, lag_sem,
    ) = rest
    b = lax.axis_index("batch")
    s = lax.axis_index("seq")

    places = (
        [lax.rem(s // 16 + i, 4) * 16 for i in range(4)],
        [lax.rem(s // 8 + i, 2) * 8 for i in range(2)],
        [lax.rem(s // 2 + i, 4) * 2 for i in range(4)],
    )
    core = lax.rem(s, 2)
    own = s - core
    chips = [sum(place[i] for place, i in zip(places, shift)) for shift in SHIFTS]
    peers = [chip + i for chip in chips for i in range(2)] + [own + 1 - core]
    early = [jnp.where(own == 0, chips[0], 0)] + [jnp.where(chip == 0, chips[0], chip) for chip in chips[1:]]
    early_peers = [chip + i for chip in early for i in range(2)] + [own + 1 - core]

    barrier = pltpu.get_barrier_semaphore()
    for d in peers[:24]:
        pl.semaphore_signal(barrier, inc=1, device_id=(b, d), device_id_type=MESH)

    loads = [
        pltpu.make_async_copy(src, dst, load_sem.at[i])
        for i, (src, dst) in enumerate(
            zip(
                (key_hbm, value_hbm, query_hbm, cotangent_hbm, filters_hbm, skip_hbm)
                + tuple(table_hbm),
                (key, value, query, cotangent, filters, skip) + tuple(tables),
            )
        )
    ]
    for load in loads:
        load.start()

    for d in peers[24:]:
        pl.semaphore_signal(barrier, inc=1, device_id=(b, d), device_id_type=MESH)
    pl.semaphore_signal(barrier, inc=1, device_id=(1 - b, s), device_id_type=MESH)

    for first, second, left, right, target in (
        (0, 1, key, value, mixed_send),
        (2, 3, query, cotangent, up_send),
    ):
        loads[first].wait()
        loads[second].wait()
        for bb in range(2):
            for half in range(2):
                tokens = slice(half * 128, (half + 1) * 128)
                product = left[bb, tokens, :] * right[bb, tokens, :]
                target[pl.ds(bb * 2 + half, 128, stride=4), :] = product.T

    pl.semaphore_wait(barrier, PEERS)

    def block(i, channels):
        rows = len(channels) * PART
        return pl.ds(pl.multiple_of(i * ROWS + channels[0] * PART, rows), rows)

    def send(source, target, k, channels, partners, keep=True):
        for d in partners:
            pltpu.make_async_remote_copy(
                src_ref=source.at[block(d, channels)],
                dst_ref=target.at[block(s, channels)],
                send_sem=send_sem.at[k, channels[0]],
                recv_sem=recv_sem.at[k, channels[0]],
                device_id=(b, d),
                device_id_type=MESH,
            ).start()
        if keep:
            target[block(s, channels), :] = source[block(s, channels), :]

    def settled(source, target, k, channels):
        rows = pl.ds(0, (PEERS - 1) * PART * len(channels))
        return pltpu.make_async_remote_copy(
            src_ref=source.at[rows],
            dst_ref=target.at[rows],
            send_sem=send_sem.at[k, channels[0]],
            recv_sem=recv_sem.at[k, channels[0]],
            device_id=(1 - b, s),
            device_id_type=MESH,
        )

    for channels in MIXED_CHUNKS:
        send(mixed_send, mixed_got, 0, channels, peers)
    for channels in UP_CHUNKS:
        send(up_send, up_got, 1, channels, peers)

    for load in loads[4:]:
        load.wait()
    for c in range(2):
        for n1 in range(PEERS):
            filter_rows[c * PEERS + n1 : c * PEERS + n1 + 1, :] = filters[
                c : c + 1, n1 * K2 : (n1 + 1) * K2
            ]
    forward_filters(filter_rows, filter_spec, tables)

    def spread(results, target, channels):
        for result, c in zip(results, channels):
            for bb in range(2):
                for half in range(2):
                    lanes = slice(bb * K2 + half * 128, bb * K2 + (half + 1) * 128)
                    target[pl.ds(c * 4 + bb * 2 + half, PEERS, stride=ROWS), :] = result[:, lanes]

    for channels in MIXED_CHUNKS:
        settled(mixed_send, mixed_got, 0, channels).wait_recv()
        forward(mixed_got, mixed_spec, channels, tables)
        spread(inverse(mixed_spec, filter_spec, channels, False, tables, False), conv_send, channels)
        send(conv_send, conv_got, 2, channels, peers)
    both = (0, 1)
    settled(up_send, up_got, 1, both).wait_recv()
    forward(up_got, up_spec, both, tables)
    spread(inverse(filter_spec, up_spec, both, True, tables, False), back_send, both)
    send(back_send, back_got, 3, both, early_peers[:2], False)

    result = inverse(mixed_spec, up_spec, (0, 1), True, tables, True)
    for half in range(2):
        for c in range(2):
            lag[half, c * 32 : (c + 1) * 32, :] = result[c][half * 32 : (half + 1) * 32, :]
    lag_copy = pltpu.make_async_remote_copy(
        src_ref=lag.at[1 - b],
        dst_ref=lag_got,
        send_sem=lag_sem.at[0],
        recv_sem=lag_sem.at[1],
        device_id=(1 - b, s),
        device_id_type=MESH,
    )
    lag_copy.start()
    send(back_send, back_got, 3, both, early_peers[2:])

    gain = skip[...]
    parts = [(bb, slice(h * 128, (h + 1) * 128), pl.ds(bb * 2 + h, 128, stride=4)) for bb in range(2) for h in range(2)]
    for channels in MIXED_CHUNKS:
        settled(conv_send, conv_got, 2, channels).wait_recv()
    for bb, tokens, rows in parts:
        hidden = conv_got[rows, :].T + gain * (key[bb, tokens, :] * value[bb, tokens, :])
        output[bb, tokens, :] = query[bb, tokens, :] * hidden
        query_grad[bb, tokens, :] = cotangent[bb, tokens, :] * hidden

    lag_copy.wait_recv()
    total = (lag[b] + lag_got[...]) * (1.0 / 128.0)
    for c in range(2):
        for n in range(32):
            filter_grad[c : c + 1, n * K2 : (n + 1) * K2] = total[c * 32 + n : c * 32 + n + 1, :]
    for channels in MIXED_CHUNKS:
        settled(mixed_send, mixed_got, 0, channels).wait_send()
        settled(conv_send, conv_got, 2, channels).wait_send()
    for channels in UP_CHUNKS:
        settled(up_send, up_got, 1, channels).wait_send()
    lag_copy.wait_send()

    for channels in UP_CHUNKS:
        settled(back_send, back_got, 3, channels).wait_recv()
    for bb, tokens, rows in parts:
        mixed_grad = back_got[rows, :].T + gain * (cotangent[bb, tokens, :] * query[bb, tokens, :])
        key_grad[bb, tokens, :] = mixed_grad * value[bb, tokens, :]
        value_grad[bb, tokens, :] = mixed_grad * key[bb, tokens, :]
    for channels in UP_CHUNKS:
        settled(back_send, back_got, 3, channels).wait_send()


def store_kernel(*refs):
    sources, targets, sem = refs[:5], refs[5:10], refs[10]
    copies = []
    for i in range(5):
        for half in range(2):
            part = (half,) if i < 4 else (slice(None), pl.ds(half * 16 * K2, 16 * K2))
            copies.append(
                pltpu.make_async_copy(sources[i].at[part], targets[i].at[part], sem.at[i, half])
            )
    for copy in copies:
        copy.start()
    for copy in copies:
        copy.wait()


def per_device(query, key, value, filters, skip, cotangent):
    tables = [jnp.asarray(t) for t in make_tables()]
    message = (PEERS * ROWS, 128)
    in_hbm = pl.BlockSpec(memory_space=pltpu.HBM)
    vmem = pltpu.VMEM
    tokens = query.shape
    operands = (query, key, value, cotangent, filters, skip.reshape(1, -1), *tables)
    block = jax.ShapeDtypeStruct(tokens, F32)
    shapes = (block, block, block, block, jax.ShapeDtypeStruct((2, 32 * K2), F32))
    results = pl.pallas_call(
        main_kernel,
        out_shape=shapes,
        in_specs=[in_hbm] * len(operands),
        out_specs=(pl.BlockSpec(memory_space=pltpu.VMEM),) * 5,
        scratch_shapes=[vmem(tokens, F32)] * 4
        + [vmem(filters.shape, F32), vmem((1, tokens[2]), F32)]
        + [vmem(t.shape, t.dtype) for t in tables]
        + [vmem(message, F32)] * 8
        + [vmem((2 * PEERS, K2), F32)]
        + [vmem((2 * K1, 2 * K2), F32)] * 3
        + [vmem((2, 64, K2), F32), vmem((64, K2), F32)]
        + [
            pltpu.SemaphoreType.DMA((len(operands),)),
            pltpu.SemaphoreType.DMA((4, 2)),
            pltpu.SemaphoreType.DMA((4, 2)),
            pltpu.SemaphoreType.DMA((2,)),
        ],
        compiler_params=pltpu.CompilerParams(
            collective_id=0, has_side_effects=True, vmem_limit_bytes=40 * 1024 * 1024
        ),
        name="spectral_exchange",
    )(*[pltpu.with_memory_space_constraint(x, pltpu.HBM) for x in operands])
    return pl.pallas_call(
        store_kernel,
        out_shape=shapes,
        in_specs=[pl.BlockSpec(memory_space=pltpu.VMEM)] * 5,
        out_specs=(in_hbm,) * 5,
        scratch_shapes=[pltpu.SemaphoreType.DMA((5, 2))],
        compiler_params=pltpu.CompilerParams(vmem_limit_bytes=16 * 1024 * 1024),
        name="store",
    )(*results)


def solution(mesh):
    rows = P("batch", "seq", None)
    return jax.shard_map(
        per_device,
        mesh=mesh,
        in_specs=(rows, rows, rows, P("seq", None), P(), rows),
        out_specs=(rows, rows, rows, rows, P("seq", "batch")),
        check_vma=False,
    )
```
